256 devices in a mesh: ka: 16 (over x_lo, y, core), pw: 16 (over z, x_hi).
Axes of the slice: x: 4 (x_hi: 2, x_lo: 2; x = x_hi * 2 + x_lo), y: 4, z: 8, core: 2. Of those that a mesh axis runs over, the one named last changes fastest.
Arguments:
- coeffs: bfloat16 [256, 2, 6144, 256], P('ka', None, 'pw'), may hold values from -1.75 to 1.75
- neighbour: int32 [256], P('ka'), may hold values from 0 to 255, as said below
- gshift: int32 [6144], replicated, may hold values from 0 to 6143, each once
Outputs:
- inner_products: float32 [256, 256, 2, 256], P('pw', 'ka')
The draws below stay inside these ranges and needn't reach their ends.
Inputs may be any that keep to these rules, and one draw needn't show every extreme that they name: neighbour[k] lies in the slab of 16 k-points that starts 2 * 16 points after the start of the slab of k, counted cyclically over the 256 points; the neighbours of one slab's points are distinct. `gshift`: each row appears once.
All inputs are finite; a program needn't handle non-finite values.
Results may differ from the reference program's by a relative error of at most 0.0003.
Values may be sent and summed in bfloat16 or wider, within the bound.
No kernel may reach another device: no remote copies, remote signals or barrier semaphores. Data moves between devices by JAX's collectives and lax.ppermute only.
A program may use at most 128 MiB of HBM per device.

```python
import jax
import jax.numpy as jnp
from jax import lax

NB = 256
K_DEV = 16
SHIFT_DEV = 2
K = 256
PW = 6144
N_KA = 16


def draw_neighbour(key, part):
    slab_total = K // K_DEV
    slab_keys = jax.random.split(key, slab_total)
    orders = jax.vmap(lambda single_key: jax.random.permutation(single_key, K_DEV))(slab_keys)
    target = (jnp.arange(slab_total, dtype=jnp.int32) + SHIFT_DEV) % slab_total
    return (target[:, None] * K_DEV + orders.astype(jnp.int32)).reshape(K).astype(jnp.int32)


def block_scale(own_key, dims, cuts, low, top_value):
    def one(position, shards_of):
        steps = jax.random.uniform(jax.random.fold_in(jax.random.fold_in(own_key, 6), position), (shards_of,), jnp.float32, low / len(cuts), top_value / len(cuts))
        return jnp.repeat(jnp.exp(steps), dims[position] // shards_of).reshape((-1,) + (1,) * (len(dims) - position - 1))

    loudness = one(*cuts[0])
    for cut in cuts[1:]:
        loudness = loudness * one(*cut)
    return loudness


def scatter_about(rng, shape, scale, limit, cuts=(), kind=jnp.bfloat16):
    array = scale * jax.random.normal(rng, shape, jnp.float32)
    if cuts:
        array = array * block_scale(rng, shape, cuts, -0.22, 0.18)
    return jnp.clip(array, -limit, limit).astype(kind)


def setup_inputs(seed: int = 0) -> dict:
    streams_of = jax.random.split(jax.random.key(seed), 4)
    return {
        "coeffs": scatter_about(streams_of[0], (K, 2, PW, NB), (PW ** -0.25), 1.75, ((0, 16), (2, 16))),
        "neighbour": draw_neighbour(jax.random.fold_in(streams_of[3], 71), 0),
        "gshift": jax.random.permutation(streams_of[2], PW).astype(jnp.int32),
    }


def pair_single(own_block, partner_block):
    products_all = jnp.einsum("cgm,dgn->cdmn", own_block.astype(jnp.float32), partner_block.astype(jnp.float32), precision=lax.Precision.HIGHEST)
    real_part = products_all[0, 0] + products_all[1, 1]
    imag_part = products_all[0, 1] - products_all[1, 0]
    return jnp.stack([real_part, imag_part], axis=1)


def reference(coeffs, neighbour, gshift):
    def single(point):
        own_block = coeffs[point]
        partner_block = coeffs[neighbour[point]]
        permuted = jnp.take(partner_block, gshift, axis=1)
        wrapped = point // K_DEV >= N_KA - SHIFT_DEV
        partner_block = jnp.where(wrapped, permuted, partner_block)
        return pair_single(own_block, partner_block)

    result = lax.map(single, jnp.arange(K, dtype=jnp.int32))
    return jnp.transpose(result, (1, 0, 2, 3))
```

```python
import jax
import jax.numpy as jnp
from jax import lax
from jax.experimental import pallas as pl
from jax.experimental.pallas import tpu as pltpu
from jax.sharding import PartitionSpec as P

SHIFT_DEV = 2


def reorder_kernel(order, source, result, sems):
    count = result.shape[0]

    def block(i):
        return pltpu.make_async_copy(source.at[order[i]], result.at[i], sems.at[i])

    for i in range(count):
        block(i).start()
    for i in range(count):
        block(i).wait()


def reordered(source, order):
    return pl.pallas_call(
        reorder_kernel,
        grid_spec=pltpu.PrefetchScalarGridSpec(
            num_scalar_prefetch=1,
            grid=(),
            in_specs=[pl.BlockSpec(memory_space=pl.ANY)],
            out_specs=pl.BlockSpec(memory_space=pl.ANY),
            scratch_shapes=[pltpu.SemaphoreType.DMA((source.shape[0],))],
        ),
        out_shape=jax.ShapeDtypeStruct(source.shape, source.dtype),
        cost_estimate=pl.CostEstimate(flops=0, bytes_accessed=2 * source.size * 2, transcendentals=0),
    )(order, source)


def scatter_rows_kernel(target_ref, own_ref, out_ref):
    sources, parts, rows, bands = own_ref.shape
    height = out_ref.shape[1]
    first = pl.program_id(0) * height
    pair = 2
    wanted = first + lax.broadcasted_iota(jnp.int32, (height, pair * rows), 0)
    totals = [jnp.zeros((height, bands), jnp.float32) for _ in range(parts)]
    for s in range(0, sources, pair):
        hot = (target_ref[:, s * rows : (s + pair) * rows] == wanted).astype(jnp.bfloat16)
        for c in range(parts):
            block = own_ref[s : s + pair, c].reshape(pair * rows, bands)
            totals[c] += jnp.dot(hot, block, preferred_element_type=jnp.float32)
    for c in range(parts):
        out_ref[c] = totals[c].astype(out_ref.dtype)


def scattered_rows(own, target):
    sources, parts, rows, bands = own.shape
    total = sources * rows
    height = 256
    return pl.pallas_call(
        scatter_rows_kernel,
        grid=(total // height,),
        in_specs=[
            pl.BlockSpec((1, total), lambda i: (0, 0)),
            pl.BlockSpec(own.shape, lambda i: (0, 0, 0, 0), pipeline_mode=pl.Buffered(1)),
        ],
        out_specs=pl.BlockSpec((parts, height, bands), lambda i: (0, i, 0)),
        out_shape=jax.ShapeDtypeStruct((parts, total, bands), own.dtype),
        compiler_params=pltpu.CompilerParams(vmem_limit_bytes=40 << 20),
        cost_estimate=pl.CostEstimate(
            flops=2 * total * total * parts * bands, bytes_accessed=4 * own.size, transcendentals=0
        ),
    )(target.reshape(1, total), own)


def pair_kernel(own_ref, partner_ref, out_ref, acc_ref):
    step = pl.program_id(0)

    @pl.when(step == 0)
    def _():
        acc_ref[...] = jnp.zeros_like(acc_ref)

    sources, parts, rows, bands = partner_ref.shape
    own = [own_ref[c] for c in range(2)]
    partner = [partner_ref[:, d].reshape(sources * rows, bands) for d in range(2)]

    def product(c, d):
        return lax.dot_general(
            own[c], partner[d], (((0,), (0,)), ((), ())), preferred_element_type=jnp.float32
        )

    acc_ref[0] += product(0, 0) + product(1, 1)
    acc_ref[1] += product(0, 1) - product(1, 0)

    @pl.when(step == pl.num_programs(0) - 1)
    def _():
        for d in range(2):
            out_ref[:, d * bands : (d + 1) * bands] = acc_ref[d]


def pair_products(own, partner):
    sources, parts, rows, bands = partner.shape
    take = 2
    return pl.pallas_call(
        pair_kernel,
        grid=(sources // take,),
        in_specs=[
            pl.BlockSpec((parts, take * rows, bands), lambda i: (0, i, 0)),
            pl.BlockSpec((take, parts, rows, bands), lambda i: (i, 0, 0, 0)),
        ],
        out_specs=pl.BlockSpec((bands, 2 * bands), lambda i: (0, 0)),
        out_shape=jax.ShapeDtypeStruct((bands, 2 * bands), jnp.float32),
        scratch_shapes=[pltpu.VMEM((2, bands, bands), jnp.float32)],
        compiler_params=pltpu.CompilerParams(vmem_limit_bytes=40 << 20),
        cost_estimate=pl.CostEstimate(
            flops=8 * sources * rows * bands * bands, bytes_accessed=4 * partner.size, transcendentals=0
        ),
    )(own, partner)


def on_device(coeffs, neighbour, gshift):
    slab_points, parts, rows, bands = coeffs.shape
    ka_count = lax.axis_size("ka")
    wrapped = lax.axis_index("ka") >= ka_count - SHIFT_DEV
    route = [((i + SHIFT_DEV) % ka_count, i) for i in range(ka_count)]
    arrived = lax.ppermute(coeffs, "ka", route)
    own = lax.all_to_all(coeffs, "pw", split_axis=0, concat_axis=0, tiled=True)
    partner = reordered(arrived, neighbour % slab_points)
    partner = lax.all_to_all(partner, "pw", split_axis=0, concat_axis=0, tiled=True)
    target = jnp.where(wrapped, gshift, lax.iota(jnp.int32, gshift.shape[0]))
    products = pair_products(scattered_rows(own, target), partner)
    products = lax.all_to_all(products, "pw", split_axis=0, concat_axis=0, tiled=True)
    products = products.reshape(slab_points, bands // slab_points, 2, bands)
    return jnp.transpose(products, (1, 0, 2, 3))


def solution(mesh):
    placed = (P("ka", None, "pw", None), P("ka"), P())
    return jax.shard_map(
        on_device, mesh=mesh, in_specs=placed, out_specs=P("pw", "ka", None, None), check_vma=False
    )
```

```python
import jax
import jax.numpy as jnp
from jax import lax
from jax.experimental import pallas as pl
from jax.experimental.pallas import tpu as pltpu
from jax.sharding import PartitionSpec as P

SHIFT_DEV = 2


def reorder_kernel(order, source, result):
    result[...] = source[...]


def reordered(source, order):
    block = (1,) + source.shape[1:]
    return pl.pallas_call(
        reorder_kernel,
        grid_spec=pltpu.PrefetchScalarGridSpec(
            num_scalar_prefetch=1,
            grid=(source.shape[0],),
            in_specs=[pl.BlockSpec(block, lambda i, order: (order[i], 0, 0))],
            out_specs=pl.BlockSpec(block, lambda i, order: (i, 0, 0)),
        ),
        out_shape=jax.ShapeDtypeStruct(source.shape, source.dtype),
        cost_estimate=pl.CostEstimate(flops=0, bytes_accessed=4 * source.size, transcendentals=0),
    )(order, source)


def scatter_rows_kernel(target_ref, own_ref, out_ref):
    sources, parts, rows, bands = own_ref.shape
    height = out_ref.shape[1]
    first = pl.program_id(0) * height
    pair = 2
    wanted = first + lax.broadcasted_iota(jnp.int32, (height, pair * rows), 0)
    totals = [jnp.zeros((height, bands), jnp.float32) for _ in range(parts)]
    for s in range(0, sources, pair):
        hot = (target_ref[:, s * rows : (s + pair) * rows] == wanted).astype(jnp.bfloat16)
        for c in range(parts):
            block = own_ref[s : s + pair, c].reshape(pair * rows, bands)
            totals[c] += jnp.dot(hot, block, preferred_element_type=jnp.float32)
    for c in range(parts):
        out_ref[c] = totals[c].astype(out_ref.dtype)


def scattered_rows(own, target):
    sources, parts, rows, bands = own.shape
    total = sources * rows
    height = 256
    return pl.pallas_call(
        scatter_rows_kernel,
        grid=(total // height,),
        in_specs=[
            pl.BlockSpec((1, total), lambda i: (0, 0)),
            pl.BlockSpec(own.shape, lambda i: (0, 0, 0, 0), pipeline_mode=pl.Buffered(1)),
        ],
        out_specs=pl.BlockSpec((parts, height, bands), lambda i: (0, i, 0)),
        out_shape=jax.ShapeDtypeStruct((parts, total, bands), own.dtype),
        compiler_params=pltpu.CompilerParams(vmem_limit_bytes=40 << 20),
        cost_estimate=pl.CostEstimate(
            flops=2 * total * total * parts * bands, bytes_accessed=4 * own.size, transcendentals=0
        ),
    )(target.reshape(1, total), own)


def plane_products(own_ref, partner_ref):
    sources, rows, bands = partner_ref.shape
    partner = partner_ref[...].reshape(sources * rows, bands)
    return [
        lax.dot_general(
            own_ref[c], partner, (((0,), (0,)), ((), ())), preferred_element_type=jnp.float32
        )
        for c in range(2)
    ]


def first_plane_kernel(own_ref, partner_ref, out_ref):
    @pl.when(pl.program_id(0) == 0)
    def _():
        out_ref[...] = jnp.zeros_like(out_ref)

    real, imag = plane_products(own_ref, partner_ref)
    out_ref[0] += real
    out_ref[1] -= imag


def second_plane_kernel(own_ref, partner_ref, first_ref, out_ref, acc_ref):
    step = pl.program_id(0)

    @pl.when(step == 0)
    def _():
        acc_ref[...] = first_ref[...]

    imag, real = plane_products(own_ref, partner_ref)
    acc_ref[0] += real
    acc_ref[1] += imag

    @pl.when(step == pl.num_programs(0) - 1)
    def _():
        bands = acc_ref.shape[1]
        for d in range(2):
            out_ref[:, d * bands : (d + 1) * bands] = acc_ref[d]


TAKE = 2


def pair_specs(own, partner):
    sources, rows, bands = partner.shape
    specs = [
        pl.BlockSpec((own.shape[0], TAKE * rows, bands), lambda i: (0, i, 0)),
        pl.BlockSpec((TAKE, rows, bands), lambda i: (i, 0, 0)),
    ]
    cost = pl.CostEstimate(
        flops=4 * sources * rows * bands * bands, bytes_accessed=6 * partner.size, transcendentals=0
    )
    return (sources // TAKE,), specs, cost


def first_plane(own, partner):
    grid, specs, cost = pair_specs(own, partner)
    bands = own.shape[-1]
    return pl.pallas_call(
        first_plane_kernel,
        grid=grid,
        in_specs=specs,
        out_specs=pl.BlockSpec((2, bands, bands), lambda i: (0, 0, 0)),
        out_shape=jax.ShapeDtypeStruct((2, bands, bands), jnp.float32),
        compiler_params=pltpu.CompilerParams(vmem_limit_bytes=32 << 20),
        cost_estimate=cost,
    )(own, partner)


def second_plane(own, partner, first):
    grid, specs, cost = pair_specs(own, partner)
    bands = own.shape[-1]
    return pl.pallas_call(
        second_plane_kernel,
        grid=grid,
        in_specs=specs + [pl.BlockSpec(first.shape, lambda i: (0, 0, 0))],
        out_specs=pl.BlockSpec((bands, 2 * bands), lambda i: (0, 0)),
        out_shape=jax.ShapeDtypeStruct((bands, 2 * bands), jnp.float32),
        scratch_shapes=[pltpu.VMEM(first.shape, jnp.float32)],
        compiler_params=pltpu.CompilerParams(vmem_limit_bytes=32 << 20),
        cost_estimate=cost,
    )(own, partner, first)


def on_device(coeffs, neighbour, gshift):
    slab_points, parts, rows, bands = coeffs.shape
    ka_count = lax.axis_size("ka")
    wrapped = lax.axis_index("ka") >= ka_count - SHIFT_DEV
    route = [((i + SHIFT_DEV) % ka_count, i) for i in range(ka_count)]

    def spread(block):
        return lax.all_to_all(block, "pw", split_axis=0, concat_axis=0, tiled=True)

    order = neighbour % slab_points
    own = spread(coeffs)
    arrived = [lax.ppermute(coeffs[:, c], "ka", route) for c in range(parts)]
    waiting = [reordered(plane, order) for plane in arrived]
    own, waiting[0] = lax.optimization_barrier((own, waiting[0]))
    real = spread(waiting[0])
    target = jnp.where(wrapped, gshift, lax.iota(jnp.int32, gshift.shape[0]))
    moved = scattered_rows(own, target)
    real, moved, waiting[1] = lax.optimization_barrier((real, moved, waiting[1]))
    imag = spread(waiting[1])
    first = first_plane(moved, real)
    products = second_plane(moved, imag, first)
    products = spread(products).reshape(slab_points, bands // slab_points, 2, bands)
    return jnp.transpose(products, (1, 0, 2, 3))


def solution(mesh):
    placed = (P("ka", None, "pw", None), P("ka"), P())
    return jax.shard_map(
        on_device, mesh=mesh, in_specs=placed, out_specs=P("pw", "ka", None, None), check_vma=False
    )
```

```python
import jax
import jax.numpy as jnp
from jax import lax
from jax.experimental import pallas as pl
from jax.experimental.pallas import tpu as pltpu
from jax.sharding import PartitionSpec as P

SHIFT_DEV = 2


def reorder_kernel(order, source, result, held, read, written):
    count = result.shape[0]

    def fetch(i):
        return pltpu.make_async_copy(source.at[order[i]], held.at[i], read.at[i])

    def store(i):
        return pltpu.make_async_copy(held.at[i], result.at[i], written.at[i])

    for i in range(count):
        fetch(i).start()
    for i in range(count):
        fetch(i).wait()
        store(i).start()
    for i in range(count):
        store(i).wait()


def reordered(source, order):
    count = source.shape[0]
    return pl.pallas_call(
        reorder_kernel,
        grid_spec=pltpu.PrefetchScalarGridSpec(
            num_scalar_prefetch=1,
            grid=(),
            in_specs=[pl.BlockSpec(memory_space=pltpu.HBM)],
            out_specs=pl.BlockSpec(memory_space=pltpu.HBM),
            scratch_shapes=[
                pltpu.VMEM(source.shape, source.dtype),
                pltpu.SemaphoreType.DMA((count,)),
                pltpu.SemaphoreType.DMA((count,)),
            ],
        ),
        out_shape=jax.ShapeDtypeStruct(source.shape, source.dtype),
        compiler_params=pltpu.CompilerParams(vmem_limit_bytes=32 << 20),
        cost_estimate=pl.CostEstimate(flops=0, bytes_accessed=4 * source.size, transcendentals=0),
    )(order, source)


def scatter_rows_kernel(target_ref, own_ref, out_ref):
    sources, parts, rows, bands = own_ref.shape
    height = out_ref.shape[1]
    first = pl.program_id(0) * height
    pair = 2
    wanted = first + lax.broadcasted_iota(jnp.int32, (height, pair * rows), 0)
    totals = [jnp.zeros((height, bands), jnp.float32) for _ in range(parts)]
    for s in range(0, sources, pair):
        hot = (target_ref[:, s * rows : (s + pair) * rows] == wanted).astype(jnp.bfloat16)
        for c in range(parts):
            block = own_ref[s : s + pair, c].reshape(pair * rows, bands)
            totals[c] += jnp.dot(hot, block, preferred_element_type=jnp.float32)
    for c in range(parts):
        out_ref[c] = totals[c].astype(out_ref.dtype)


def scattered_rows(own, target):
    sources, parts, rows, bands = own.shape
    total = sources * rows
    height = 256
    return pl.pallas_call(
        scatter_rows_kernel,
        grid=(total // height,),
        in_specs=[
            pl.BlockSpec((1, total), lambda i: (0, 0)),
            pl.BlockSpec(own.shape, lambda i: (0, 0, 0, 0), pipeline_mode=pl.Buffered(1)),
        ],
        out_specs=pl.BlockSpec((parts, height, bands), lambda i: (0, i, 0)),
        out_shape=jax.ShapeDtypeStruct((parts, total, bands), own.dtype),
        compiler_params=pltpu.CompilerParams(vmem_limit_bytes=40 << 20),
        cost_estimate=pl.CostEstimate(
            flops=2 * total * total * parts * bands, bytes_accessed=4 * own.size, transcendentals=0
        ),
    )(target.reshape(1, total), own)


def plane_products(own_ref, partner_ref):
    sources, rows, bands = partner_ref.shape
    partner = partner_ref[...].reshape(sources * rows, bands)
    return [
        lax.dot_general(
            own_ref[c], partner, (((0,), (0,)), ((), ())), preferred_element_type=jnp.float32
        )
        for c in range(2)
    ]


def first_plane_kernel(own_ref, partner_ref, out_ref):
    @pl.when(pl.program_id(0) == 0)
    def _():
        out_ref[...] = jnp.zeros_like(out_ref)

    real, imag = plane_products(own_ref, partner_ref)
    out_ref[0] += real
    out_ref[1] -= imag


def second_plane_kernel(own_ref, partner_ref, first_ref, out_ref, acc_ref):
    step = pl.program_id(0)

    @pl.when(step == 0)
    def _():
        acc_ref[...] = first_ref[...]

    imag, real = plane_products(own_ref, partner_ref)
    acc_ref[0] += real
    acc_ref[1] += imag

    @pl.when(step == pl.num_programs(0) - 1)
    def _():
        bands = acc_ref.shape[1]
        for d in range(2):
            out_ref[:, d * bands : (d + 1) * bands] = acc_ref[d]


TAKE = 2


def pair_specs(own, partner):
    sources, rows, bands = partner.shape
    specs = [
        pl.BlockSpec((own.shape[0], TAKE * rows, bands), lambda i: (0, i, 0)),
        pl.BlockSpec((TAKE, rows, bands), lambda i: (i, 0, 0)),
    ]
    cost = pl.CostEstimate(
        flops=4 * sources * rows * bands * bands, bytes_accessed=6 * partner.size, transcendentals=0
    )
    return (sources // TAKE,), specs, cost


def first_plane(own, partner):
    grid, specs, cost = pair_specs(own, partner)
    bands = own.shape[-1]
    return pl.pallas_call(
        first_plane_kernel,
        grid=grid,
        in_specs=specs,
        out_specs=pl.BlockSpec((2, bands, bands), lambda i: (0, 0, 0)),
        out_shape=jax.ShapeDtypeStruct((2, bands, bands), jnp.float32),
        compiler_params=pltpu.CompilerParams(vmem_limit_bytes=32 << 20),
        cost_estimate=cost,
    )(own, partner)


def second_plane(own, partner, first):
    grid, specs, cost = pair_specs(own, partner)
    bands = own.shape[-1]
    return pl.pallas_call(
        second_plane_kernel,
        grid=grid,
        in_specs=specs + [pl.BlockSpec(first.shape, lambda i: (0, 0, 0))],
        out_specs=pl.BlockSpec((bands, 2 * bands), lambda i: (0, 0)),
        out_shape=jax.ShapeDtypeStruct((bands, 2 * bands), jnp.float32),
        scratch_shapes=[pltpu.VMEM(first.shape, jnp.float32)],
        compiler_params=pltpu.CompilerParams(vmem_limit_bytes=32 << 20),
        cost_estimate=cost,
    )(own, partner, first)


def on_device(coeffs, neighbour, gshift):
    slab_points, parts, rows, bands = coeffs.shape
    ka_count = lax.axis_size("ka")
    wrapped = lax.axis_index("ka") >= ka_count - SHIFT_DEV
    route = [((i + SHIFT_DEV) % ka_count, i) for i in range(ka_count)]

    def spread(block):
        return lax.all_to_all(block, "pw", split_axis=0, concat_axis=0, tiled=True)

    order = neighbour % slab_points
    own = spread(coeffs)
    arrived = [lax.ppermute(coeffs[:, c], "ka", route) for c in range(parts)]
    waiting = reordered(arrived[0], order)
    own, waiting = lax.optimization_barrier((own, waiting))
    real = spread(waiting)
    target = jnp.where(wrapped, gshift, lax.iota(jnp.int32, gshift.shape[0]))
    moved = pltpu.with_memory_space_constraint(scattered_rows(own, target), pltpu.HBM)
    moved, late = lax.optimization_barrier((moved, arrived[1]))
    waiting = reordered(late, order)
    real, waiting = lax.optimization_barrier((real, waiting))
    imag = spread(waiting)
    first = first_plane(moved, real)
    products = second_plane(moved, imag, first)
    products = spread(products).reshape(slab_points, bands // slab_points, 2, bands)
    return jnp.transpose(products, (1, 0, 2, 3))


def solution(mesh):
    placed = (P("ka", None, "pw", None), P("ka"), P())
    return jax.shard_map(
        on_device, mesh=mesh, in_specs=placed, out_specs=P("pw", "ka", None, None), check_vma=False
    )
```

```python
import jax
import jax.numpy as jnp
from jax import lax
from jax.experimental import pallas as pl
from jax.experimental.pallas import tpu as pltpu
from jax.sharding import PartitionSpec as P

SHIFT_DEV = 2


def reorder_kernel(order, relayed, *refs):
    *sources, result, held, read, written = refs
    count = result.shape[0]

    def fetch(source, i):
        return pltpu.make_async_copy(source.at[order[i]], held.at[i], read.at[i])

    def store(i):
        return pltpu.make_async_copy(held.at[i], result.at[i], written.at[i])

    for choice, source in enumerate(sources):

        @pl.when(relayed[0] == choice)
        def _(source=source):
            for i in range(count):
                fetch(source, i).start()
            for i in range(count):
                fetch(source, i).wait()
                store(i).start()

    for i in range(count):
        store(i).wait()


def reordered(order, relayed, *sources):
    shape, dtype = sources[0].shape, sources[0].dtype
    count = shape[0]
    return pl.pallas_call(
        reorder_kernel,
        grid_spec=pltpu.PrefetchScalarGridSpec(
            num_scalar_prefetch=2,
            grid=(),
            in_specs=[pl.BlockSpec(memory_space=pltpu.HBM)] * len(sources),
            out_specs=pl.BlockSpec(memory_space=pltpu.HBM),
            scratch_shapes=[
                pltpu.VMEM(shape, dtype),
                pltpu.SemaphoreType.DMA((count,)),
                pltpu.SemaphoreType.DMA((count,)),
            ],
        ),
        out_shape=jax.ShapeDtypeStruct(shape, dtype),
        compiler_params=pltpu.CompilerParams(vmem_limit_bytes=56 << 20),
        cost_estimate=pl.CostEstimate(flops=0, bytes_accessed=4 * sources[0].size, transcendentals=0),
    )(order, relayed, *sources)


def scatter_rows_kernel(target_ref, own_ref, out_ref):
    sources, parts, rows, bands = own_ref.shape
    height = out_ref.shape[1]
    first = pl.program_id(0) * height
    pair = 2
    wanted = first + lax.broadcasted_iota(jnp.int32, (height, pair * rows), 0)
    totals = [jnp.zeros((height, bands), jnp.float32) for _ in range(parts)]
    for s in range(0, sources, pair):
        hot = (target_ref[:, s * rows : (s + pair) * rows] == wanted).astype(jnp.bfloat16)
        for c in range(parts):
            block = own_ref[s : s + pair, c].reshape(pair * rows, bands)
            totals[c] += jnp.dot(hot, block, preferred_element_type=jnp.float32)
    for c in range(parts):
        out_ref[c] = totals[c].astype(out_ref.dtype)


def scattered_rows(own, target):
    sources, parts, rows, bands = own.shape
    total = sources * rows
    height = 256
    return pl.pallas_call(
        scatter_rows_kernel,
        grid=(total // height,),
        in_specs=[
            pl.BlockSpec((1, total), lambda i: (0, 0)),
            pl.BlockSpec(own.shape, lambda i: (0, 0, 0, 0), pipeline_mode=pl.Buffered(1)),
        ],
        out_specs=pl.BlockSpec((parts, height, bands), lambda i: (0, i, 0)),
        out_shape=jax.ShapeDtypeStruct((parts, total, bands), own.dtype),
        compiler_params=pltpu.CompilerParams(vmem_limit_bytes=56 << 20),
        cost_estimate=pl.CostEstimate(
            flops=2 * total * total * parts * bands, bytes_accessed=4 * own.size, transcendentals=0
        ),
    )(target.reshape(1, total), own)


def plane_products(own_ref, partner_ref):
    sources, rows, bands = partner_ref.shape
    partner = partner_ref[...].reshape(sources * rows, bands)
    return [
        lax.dot_general(
            own_ref[c], partner, (((0,), (0,)), ((), ())), preferred_element_type=jnp.float32
        )
        for c in range(2)
    ]


def first_plane_kernel(own_ref, partner_ref, out_ref):
    @pl.when(pl.program_id(0) == 0)
    def _():
        out_ref[...] = jnp.zeros_like(out_ref)

    real, imag = plane_products(own_ref, partner_ref)
    out_ref[0] += real
    out_ref[1] -= imag


def second_plane_kernel(own_ref, partner_ref, first_ref, out_ref, acc_ref):
    step = pl.program_id(0)

    @pl.when(step == 0)
    def _():
        acc_ref[...] = first_ref[...]

    imag, real = plane_products(own_ref, partner_ref)
    acc_ref[0] += real
    acc_ref[1] += imag

    @pl.when(step == pl.num_programs(0) - 1)
    def _():
        bands = acc_ref.shape[1]
        for d in range(2):
            out_ref[:, d * bands : (d + 1) * bands] = acc_ref[d]


TAKE = 2


def pair_specs(own, partner):
    sources, rows, bands = partner.shape
    specs = [
        pl.BlockSpec((own.shape[0], TAKE * rows, bands), lambda i: (0, i, 0)),
        pl.BlockSpec((TAKE, rows, bands), lambda i: (i, 0, 0)),
    ]
    cost = pl.CostEstimate(
        flops=4 * sources * rows * bands * bands, bytes_accessed=6 * partner.size, transcendentals=0
    )
    return (sources // TAKE,), specs, cost


def first_plane(own, partner):
    grid, specs, cost = pair_specs(own, partner)
    bands = own.shape[-1]
    return pl.pallas_call(
        first_plane_kernel,
        grid=grid,
        in_specs=specs,
        out_specs=pl.BlockSpec((2, bands, bands), lambda i: (0, 0, 0)),
        out_shape=jax.ShapeDtypeStruct((2, bands, bands), jnp.float32),
        compiler_params=pltpu.CompilerParams(vmem_limit_bytes=32 << 20),
        cost_estimate=cost,
    )(own, partner)


def second_plane(own, partner, first):
    grid, specs, cost = pair_specs(own, partner)
    bands = own.shape[-1]
    return pl.pallas_call(
        second_plane_kernel,
        grid=grid,
        in_specs=specs + [pl.BlockSpec(first.shape, lambda i: (0, 0, 0))],
        out_specs=pl.BlockSpec((bands, 2 * bands), lambda i: (0, 0)),
        out_shape=jax.ShapeDtypeStruct((bands, 2 * bands), jnp.float32),
        scratch_shapes=[pltpu.VMEM(first.shape, jnp.float32)],
        compiler_params=pltpu.CompilerParams(vmem_limit_bytes=32 << 20),
        cost_estimate=cost,
    )(own, partner, first)


def on_device(coeffs, neighbour, gshift):
    slab_points, parts, rows, bands = coeffs.shape
    ka_count = lax.axis_size("ka")
    here = lax.axis_index("ka")
    wrapped = here >= ka_count - SHIFT_DEV
    half = ka_count // 2
    crosses = here % half >= half - SHIFT_DEV

    def spread(block):
        return lax.all_to_all(block, "pw", split_axis=0, concat_axis=0, tiled=True)

    order = neighbour % slab_points
    own = spread(coeffs)
    straight = [((i + SHIFT_DEV) % ka_count, i) for i in range(ka_count)]
    around = [(i // half * half + (i + SHIFT_DEV) % half, i) for i in range(ka_count)]
    swap = [((i + half) % ka_count, i) for i in range(ka_count) if i % half >= half - SHIFT_DEV]
    direct = lax.ppermute(coeffs[:, 0], "ka", straight)
    turned = lax.ppermute(coeffs[:, 1], "ka", around)
    waiting = reordered(order, jnp.zeros((1,), jnp.int32), direct)
    own, waiting, turned = lax.optimization_barrier((own, waiting, turned))
    swapped = lax.ppermute(turned, "ka", swap)
    real = spread(waiting)
    target = jnp.where(wrapped, gshift, lax.iota(jnp.int32, gshift.shape[0]))
    moved = pltpu.with_memory_space_constraint(scattered_rows(own, target), pltpu.HBM)
    moved, swapped = lax.optimization_barrier((moved, swapped))
    waiting = reordered(order, crosses.astype(jnp.int32).reshape(1), turned, swapped)
    real, waiting = lax.optimization_barrier((real, waiting))
    imag = spread(waiting)
    first = first_plane(moved, real)
    products = second_plane(moved, imag, first)
    products = spread(products).reshape(slab_points, bands // slab_points, 2, bands)
    return jnp.transpose(products, (1, 0, 2, 3))


def solution(mesh):
    placed = (P("ka", None, "pw", None), P("ka"), P())
    return jax.shard_map(
        on_device, mesh=mesh, in_specs=placed, out_specs=P("pw", "ka", None, None), check_vma=False
    )
```

```python
import jax
import jax.numpy as jnp
from jax import lax
from jax.experimental import pallas as pl
from jax.experimental.pallas import tpu as pltpu
from jax.sharding import PartitionSpec as P

SHIFT_DEV = 2


def reordered(order, relayed, *pieces):
    sources = [source for piece in pieces for source in piece]
    count, _, bands = sources[0].shape
    rows = sum(piece[0].shape[1] for piece in pieces)
    shape, dtype = (count, rows, bands), sources[0].dtype

    def kernel(order, relayed, *refs):
        *given, result, held, read, written = refs

        def fetches(choice):
            at, first, copies = 0, 0, []
            for p, piece in enumerate(pieces):
                source = given[at + min(choice, len(piece) - 1)]
                height = piece[0].shape[1]
                copies += [
                    pltpu.make_async_copy(
                        source.at[order[i]], held.at[i, pl.ds(first, height)], read.at[p, i]
                    )
                    for i in range(count)
                ]
                at, first = at + len(piece), first + height
            return copies

        stores = [
            pltpu.make_async_copy(held.at[i], result.at[i], written.at[i]) for i in range(count)
        ]
        for choice in range(max(len(piece) for piece in pieces)):

            @pl.when(relayed[0] == choice)
            def _(choice=choice):
                copies = fetches(choice)
                for copy in copies:
                    copy.start()
                for i in range(count):
                    for copy in copies[i::count]:
                        copy.wait()
                    stores[i].start()

        for store in stores:
            store.wait()

    return pl.pallas_call(
        kernel,
        grid_spec=pltpu.PrefetchScalarGridSpec(
            num_scalar_prefetch=2,
            grid=(),
            in_specs=[pl.BlockSpec(memory_space=pltpu.HBM)] * len(sources),
            out_specs=pl.BlockSpec(memory_space=pltpu.HBM),
            scratch_shapes=[
                pltpu.VMEM(shape, dtype),
                pltpu.SemaphoreType.DMA((len(pieces), count)),
                pltpu.SemaphoreType.DMA((count,)),
            ],
        ),
        out_shape=jax.ShapeDtypeStruct(shape, dtype),
        compiler_params=pltpu.CompilerParams(vmem_limit_bytes=56 << 20),
        cost_estimate=pl.CostEstimate(
            flops=0, bytes_accessed=4 * count * rows * bands, transcendentals=0
        ),
    )(order, relayed, *sources)


def scatter_rows_kernel(target_ref, own_ref, out_ref):
    sources, parts, rows, bands = own_ref.shape
    height = out_ref.shape[2]
    first = pl.program_id(0) * height
    pair = 2
    wanted = first + lax.broadcasted_iota(jnp.int32, (height, pair * rows), 0)
    totals = [jnp.zeros((height, bands), jnp.float32) for _ in range(parts)]
    for s in range(0, sources, pair):
        hot = (target_ref[:, s * rows : (s + pair) * rows] == wanted).astype(jnp.bfloat16)
        for c in range(parts):
            block = own_ref[s : s + pair, c].reshape(pair * rows, bands)
            totals[c] += jnp.dot(hot, block, preferred_element_type=jnp.float32)
    for c in range(parts):
        out_ref[c] = totals[c].T.astype(out_ref.dtype)


def scattered_rows(own, target):
    sources, parts, rows, bands = own.shape
    total = sources * rows
    height = 256
    return pl.pallas_call(
        scatter_rows_kernel,
        grid=(total // height,),
        in_specs=[
            pl.BlockSpec((1, total), lambda i: (0, 0)),
            pl.BlockSpec(own.shape, lambda i: (0, 0, 0, 0), pipeline_mode=pl.Buffered(1)),
        ],
        out_specs=pl.BlockSpec((parts, bands, height), lambda i: (0, 0, i)),
        out_shape=jax.ShapeDtypeStruct((parts, bands, total), own.dtype),
        compiler_params=pltpu.CompilerParams(vmem_limit_bytes=56 << 20),
        cost_estimate=pl.CostEstimate(
            flops=2 * total * total * parts * bands, bytes_accessed=4 * own.size, transcendentals=0
        ),
    )(target.reshape(1, total), own)


def plane_products(own_ref, partner_ref):
    sources, rows, bands = partner_ref.shape
    partner = partner_ref[...].reshape(sources * rows, bands)
    own = own_ref[...].reshape(-1, sources * rows)
    both = jnp.dot(own, partner, preferred_element_type=jnp.float32)
    return both[:bands], both[bands:]


def first_plane_kernel(own_ref, partner_ref, out_ref):
    @pl.when(pl.program_id(0) == 0)
    def _():
        out_ref[...] = jnp.zeros_like(out_ref)

    real, imag = plane_products(own_ref, partner_ref)
    out_ref[0] += real
    out_ref[1] -= imag


def second_plane_kernel(own_ref, partner_ref, first_ref, out_ref, acc_ref):
    step = pl.program_id(0)

    @pl.when(step == 0)
    def _():
        acc_ref[...] = first_ref[...]

    imag, real = plane_products(own_ref, partner_ref)
    acc_ref[0] += real
    acc_ref[1] += imag

    @pl.when(step == pl.num_programs(0) - 1)
    def _():
        bands = acc_ref.shape[1]
        for d in range(2):
            out_ref[:, d * bands : (d + 1) * bands] = acc_ref[d]


TAKE = 2


def pair_specs(own, partner):
    sources, rows, bands = partner.shape
    specs = [
        pl.BlockSpec((own.shape[0], bands, TAKE * rows), lambda i: (0, 0, i)),
        pl.BlockSpec((TAKE, rows, bands), lambda i: (i, 0, 0)),
    ]
    cost = pl.CostEstimate(
        flops=4 * sources * rows * bands * bands, bytes_accessed=6 * partner.size, transcendentals=0
    )
    return (sources // TAKE,), specs, cost


def first_plane(own, partner):
    grid, specs, cost = pair_specs(own, partner)
    bands = own.shape[1]
    return pl.pallas_call(
        first_plane_kernel,
        grid=grid,
        in_specs=specs,
        out_specs=pl.BlockSpec((2, bands, bands), lambda i: (0, 0, 0)),
        out_shape=jax.ShapeDtypeStruct((2, bands, bands), jnp.float32),
        compiler_params=pltpu.CompilerParams(vmem_limit_bytes=56 << 20),
        cost_estimate=cost,
    )(own, partner)


def second_plane(own, partner, first):
    grid, specs, cost = pair_specs(own, partner)
    bands = own.shape[1]
    return pl.pallas_call(
        second_plane_kernel,
        grid=grid,
        in_specs=specs + [pl.BlockSpec(first.shape, lambda i: (0, 0, 0))],
        out_specs=pl.BlockSpec((bands, 2 * bands), lambda i: (0, 0)),
        out_shape=jax.ShapeDtypeStruct((bands, 2 * bands), jnp.float32),
        scratch_shapes=[pltpu.VMEM(first.shape, jnp.float32)],
        compiler_params=pltpu.CompilerParams(vmem_limit_bytes=56 << 20),
        cost_estimate=cost,
    )(own, partner, first)


def on_device(coeffs, neighbour, gshift):
    slab_points, parts, rows, bands = coeffs.shape
    ka_count = lax.axis_size("ka")
    here = lax.axis_index("ka")
    wrapped = here >= ka_count - SHIFT_DEV
    half = ka_count // 2
    crosses = here % half >= half - SHIFT_DEV

    def spread(block):
        return lax.all_to_all(block, "pw", split_axis=0, concat_axis=0, tiled=True)

    order = neighbour % slab_points
    own = spread(coeffs)
    straight = [((i + SHIFT_DEV) % ka_count, i) for i in range(ka_count)]
    around = [(i // half * half + (i + SHIFT_DEV) % half, i) for i in range(ka_count)]
    swap = [((i + half) % ka_count, i) for i in range(ka_count) if i % half >= half - SHIFT_DEV]
    cut = rows // 2
    direct = lax.ppermute(coeffs[:, 0], "ka", straight)
    turned = lax.ppermute(coeffs[:, 1, cut:], "ka", around)
    later = lax.ppermute(coeffs[:, 1, :cut], "ka", straight)
    waiting = reordered(order, jnp.zeros((1,), jnp.int32), [direct])
    own, waiting, turned = lax.optimization_barrier((own, waiting, turned))
    swapped = lax.ppermute(turned, "ka", swap)
    real = spread(waiting)
    target = jnp.where(wrapped, gshift, lax.iota(jnp.int32, gshift.shape[0]))
    moved = pltpu.with_memory_space_constraint(scattered_rows(own, target), pltpu.HBM)
    moved, swapped, later = lax.optimization_barrier((moved, swapped, later))
    waiting = reordered(order, crosses.astype(jnp.int32).reshape(1), [later], [turned, swapped])
    real, waiting = lax.optimization_barrier((real, waiting))
    imag = spread(waiting)
    first = first_plane(moved, real)
    products = second_plane(moved, imag, first)
    products = spread(products).reshape(slab_points, bands // slab_points, 2, bands)
    return jnp.transpose(products, (1, 0, 2, 3))


def solution(mesh):
    placed = (P("ka", None, "pw", None), P("ka"), P())
    return jax.shard_map(
        on_device, mesh=mesh, in_specs=placed, out_specs=P("pw", "ka", None, None), check_vma=False
    )
```

```python
import jax
import jax.numpy as jnp
from jax import lax
from jax.experimental import pallas as pl
from jax.experimental.pallas import tpu as pltpu
from jax.sharding import PartitionSpec as P

SHIFT_DEV = 2


def reordered(order, relayed, *pieces):
    sources = [source for piece in pieces for source in piece]
    count, _, bands = sources[0].shape
    rows = sum(piece[0].shape[1] for piece in pieces)
    shape, dtype = (count, rows, bands), sources[0].dtype

    def kernel(order, relayed, *refs):
        *given, result, held, read, written = refs

        def fetches(choice):
            at, first, copies = 0, 0, []
            for p, piece in enumerate(pieces):
                source = given[at + min(choice, len(piece) - 1)]
                height = piece[0].shape[1]
                copies += [
                    pltpu.make_async_copy(
                        source.at[order[i]], held.at[i, pl.ds(first, height)], read.at[p, i]
                    )
                    for i in range(count)
                ]
                at, first = at + len(piece), first + height
            return copies

        stores = [
            pltpu.make_async_copy(held.at[i], result.at[i], written.at[i]) for i in range(count)
        ]
        for choice in range(max(len(piece) for piece in pieces)):

            @pl.when(relayed[0] == choice)
            def _(choice=choice):
                copies = fetches(choice)
                for copy in copies:
                    copy.start()
                for i in range(count):
                    for copy in copies[i::count]:
                        copy.wait()
                    stores[i].start()

        for store in stores:
            store.wait()

    return pl.pallas_call(
        kernel,
        grid_spec=pltpu.PrefetchScalarGridSpec(
            num_scalar_prefetch=2,
            grid=(),
            in_specs=[pl.BlockSpec(memory_space=pltpu.HBM)] * len(sources),
            out_specs=pl.BlockSpec(memory_space=pltpu.HBM),
            scratch_shapes=[
                pltpu.VMEM(shape, dtype),
                pltpu.SemaphoreType.DMA((len(pieces), count)),
                pltpu.SemaphoreType.DMA((count,)),
            ],
        ),
        out_shape=jax.ShapeDtypeStruct(shape, dtype),
        compiler_params=pltpu.CompilerParams(vmem_limit_bytes=56 << 20),
        cost_estimate=pl.CostEstimate(
            flops=0, bytes_accessed=2 * count * rows * bands * dtype.itemsize, transcendentals=0
        ),
    )(order, relayed, *sources)


def scatter_rows_kernel(target_ref, real_ref, imag_ref, out_ref):
    sources, rows, bands = real_ref.shape
    height = out_ref.shape[2]
    first = pl.program_id(0) * height
    pair = 2
    wanted = first + lax.broadcasted_iota(jnp.int32, (height, pair * rows), 0)
    totals = [jnp.zeros((height, bands), jnp.float32) for _ in range(2)]
    for s in range(0, sources, pair):
        hot = (target_ref[:, s * rows : (s + pair) * rows] == wanted).astype(jnp.bfloat16)
        for c, plane in enumerate((real_ref, imag_ref)):
            block = plane[s : s + pair].reshape(pair * rows, bands)
            totals[c] += jnp.dot(hot, block, preferred_element_type=jnp.float32)
    for c in range(2):
        out_ref[c] = totals[c].T.astype(out_ref.dtype)


def scattered_rows(planes, target):
    sources, rows, bands = planes[0].shape
    total = sources * rows
    height = 256
    whole = pl.BlockSpec(planes[0].shape, lambda i: (0, 0, 0), pipeline_mode=pl.Buffered(1))
    return pl.pallas_call(
        scatter_rows_kernel,
        grid=(total // height,),
        in_specs=[pl.BlockSpec((1, total), lambda i: (0, 0)), whole, whole],
        out_specs=pl.BlockSpec((2, bands, height), lambda i: (0, 0, i)),
        out_shape=jax.ShapeDtypeStruct((2, bands, total), planes[0].dtype),
        compiler_params=pltpu.CompilerParams(vmem_limit_bytes=56 << 20),
        cost_estimate=pl.CostEstimate(
            flops=4 * total * total * bands, bytes_accessed=8 * planes[0].size, transcendentals=0
        ),
    )(target.reshape(1, total), *planes)


def ordered_planes_kernel(order, source, real, imag, held, read, written):
    count = real.shape[0]
    fetches, stores = [], []
    for c, result in enumerate((real, imag)):
        for i in range(count):
            fetches.append(
                pltpu.make_async_copy(source.at[order[i], c], held.at[c, i], read.at[c, i])
            )
            stores.append(pltpu.make_async_copy(held.at[c, i], result.at[i], written.at[c, i]))
    for copy in fetches:
        copy.start()
    for fetch, store in zip(fetches, stores):
        fetch.wait()
        store.start()
    for store in stores:
        store.wait()


def ordered_planes(source, order):
    count, parts, rows, bands = source.shape
    plane = jax.ShapeDtypeStruct((count, rows, bands), source.dtype)
    return pl.pallas_call(
        ordered_planes_kernel,
        grid_spec=pltpu.PrefetchScalarGridSpec(
            num_scalar_prefetch=1,
            grid=(),
            in_specs=[pl.BlockSpec(memory_space=pltpu.HBM)],
            out_specs=[pl.BlockSpec(memory_space=pltpu.HBM)] * 2,
            scratch_shapes=[
                pltpu.VMEM((parts, count, rows, bands), source.dtype),
                pltpu.SemaphoreType.DMA((parts, count)),
                pltpu.SemaphoreType.DMA((parts, count)),
            ],
        ),
        out_shape=[plane, plane],
        compiler_params=pltpu.CompilerParams(vmem_limit_bytes=56 << 20),
        cost_estimate=pl.CostEstimate(flops=0, bytes_accessed=4 * source.size, transcendentals=0),
    )(order, source)


def slab_kernel(own_of, own_ref, partner_ref, out_ref):
    own = [own_ref[0, c] for c in range(2)]
    partner = [partner_ref[0, d] for d in range(2)]

    def product(c, d):
        return lax.dot_general(
            own[c], partner[d], (((0,), (0,)), ((), ())), preferred_element_type=jnp.float32
        )

    groups, _, height, width = out_ref.shape
    bands = width // 2
    real = product(0, 0) + product(1, 1)
    imag = product(0, 1) - product(1, 0)
    out_ref[:, 0, :, :bands] = real.reshape(groups, height, bands)
    out_ref[:, 0, :, bands:] = imag.reshape(groups, height, bands)


def slab_products(coeffs, partner, own_of, groups):
    count, parts, rows, bands = partner.shape
    block = (1, parts, rows, bands)
    return pl.pallas_call(
        slab_kernel,
        grid_spec=pltpu.PrefetchScalarGridSpec(
            num_scalar_prefetch=1,
            grid=(count,),
            in_specs=[
                pl.BlockSpec(block, lambda j, own_of: (own_of[j], 0, 0, 0)),
                pl.BlockSpec(block, lambda j, own_of: (j, 0, 0, 0)),
            ],
            out_specs=pl.BlockSpec(
                (groups, 1, bands // groups, 2 * bands), lambda j, own_of: (0, j, 0, 0)
            ),
        ),
        out_shape=jax.ShapeDtypeStruct((groups, count, bands // groups, 2 * bands), jnp.float32),
        compiler_params=pltpu.CompilerParams(vmem_limit_bytes=56 << 20),
        cost_estimate=pl.CostEstimate(
            flops=8 * count * rows * bands * bands,
            bytes_accessed=4 * partner.size + 8 * count * bands * bands,
            transcendentals=0,
        ),
    )(own_of, coeffs, partner)


def plane_products(own_ref, partner_ref):
    sources, rows, bands = partner_ref.shape
    partner = partner_ref[...].reshape(sources * rows, bands)
    own = own_ref[...].reshape(-1, sources * rows)
    both = jnp.dot(own, partner, preferred_element_type=jnp.float32)
    return both[:bands], both[bands:]


def first_plane_kernel(own_ref, partner_ref, out_ref):
    @pl.when(pl.program_id(0) == 0)
    def _():
        out_ref[...] = jnp.zeros_like(out_ref)

    real, imag = plane_products(own_ref, partner_ref)
    out_ref[0] += real
    out_ref[1] -= imag


def second_plane_kernel(own_ref, partner_ref, first_ref, out_ref, acc_ref):
    step = pl.program_id(0)

    @pl.when(step == 0)
    def _():
        acc_ref[...] = first_ref[...]

    imag, real = plane_products(own_ref, partner_ref)
    acc_ref[0] += real
    acc_ref[1] += imag

    @pl.when(step == pl.num_programs(0) - 1)
    def _():
        bands = acc_ref.shape[1]
        for d in range(2):
            out_ref[:, d * bands : (d + 1) * bands] = acc_ref[d]


TAKE = 8


def pair_specs(own, partner):
    sources, rows, bands = partner.shape
    specs = [
        pl.BlockSpec((own.shape[0], bands, TAKE * rows), lambda i: (0, 0, i)),
        pl.BlockSpec((TAKE, rows, bands), lambda i: (i, 0, 0)),
    ]
    cost = pl.CostEstimate(
        flops=4 * sources * rows * bands * bands, bytes_accessed=6 * partner.size, transcendentals=0
    )
    return (sources // TAKE,), specs, cost


def first_plane(own, partner):
    grid, specs, cost = pair_specs(own, partner)
    bands = own.shape[1]
    return pl.pallas_call(
        first_plane_kernel,
        grid=grid,
        in_specs=specs,
        out_specs=pl.BlockSpec((2, bands, bands), lambda i: (0, 0, 0)),
        out_shape=jax.ShapeDtypeStruct((2, bands, bands), jnp.float32),
        compiler_params=pltpu.CompilerParams(vmem_limit_bytes=56 << 20),
        cost_estimate=cost,
    )(own, partner)


def second_plane(own, partner, first):
    grid, specs, cost = pair_specs(own, partner)
    bands = own.shape[1]
    return pl.pallas_call(
        second_plane_kernel,
        grid=grid,
        in_specs=specs + [pl.BlockSpec(first.shape, lambda i: (0, 0, 0))],
        out_specs=pl.BlockSpec((bands, 2 * bands), lambda i: (0, 0)),
        out_shape=jax.ShapeDtypeStruct((bands, 2 * bands), jnp.float32),
        scratch_shapes=[pltpu.VMEM(first.shape, jnp.float32)],
        compiler_params=pltpu.CompilerParams(vmem_limit_bytes=56 << 20),
        cost_estimate=cost,
    )(own, partner, first)


SIDES = 2


def on_device(coeffs, neighbour, gshift):
    slab_points, parts, rows, bands = coeffs.shape
    ka_count, pw_count = lax.axis_size("ka"), lax.axis_size("pw")
    wrapped = lax.axis_index("ka") >= ka_count - SHIFT_DEV
    side = lax.axis_index("pw") % SIDES
    points = lax.iota(jnp.int32, slab_points)

    def spread(block):
        return lax.all_to_all(block, "pw", split_axis=0, concat_axis=0, tiled=True)

    order = neighbour % slab_points
    own_of = jnp.sum(jnp.where(order[None, :] == points[:, None], points[None, :], 0), axis=1)
    inside = [(i + SHIFT_DEV, i) for i in range(ka_count - SHIFT_DEV)]
    outside = [((i + SHIFT_DEV) % ka_count, i) for i in range(ka_count - SHIFT_DEV, ka_count)]

    planes = ordered_planes(coeffs, jnp.where(wrapped, own_of, points))
    levels = pw_count // SIDES
    columns = [[z * SIDES + x for z in range(levels)] for x in range(SIDES)]
    swap = [(i, i + 1 - 2 * (i % SIDES)) for i in range(pw_count)]
    height = slab_points // 2
    half = ka_count // 2
    crossing = range(half - SHIFT_DEV, half)
    relayed = (lax.axis_index("ka") >= crossing[0]) & (lax.axis_index("ka") <= crossing[-1])
    first_leg = [(s, d + half if d in crossing else d) for s, d in inside]
    second_leg = [(d + half, d) for d in crossing]

    def part(i, block):
        own = own_of[i * height : (i + 1) * height]
        return slab_products(coeffs, block, own, levels)

    def summed(block):
        block = lax.psum_scatter(
            block, "pw", scatter_dimension=0, axis_index_groups=columns, tiled=True
        ).reshape(height, SIDES, bands // pw_count, 2 * bands)
        keep = lax.dynamic_index_in_dim(block, side, 1, keepdims=False)
        give = lax.dynamic_index_in_dim(block, 1 - side, 1, keepdims=False)
        return keep + lax.ppermute(give, "pw", swap)

    quarter = slab_points // 4
    early = lax.ppermute(coeffs[: 2 * quarter], "ka", inside)
    real = spread(planes[0])
    real, later, early, middle, turned = lax.optimization_barrier(
        (real, planes[1], early, coeffs[2 * quarter : 3 * quarter], coeffs[3 * quarter :])
    )
    imag = spread(later)
    turned = lax.ppermute(turned, "ka", first_leg)
    middle = lax.ppermute(middle, "ka", inside)
    real_over = lax.ppermute(real, "ka", outside)
    upper = part(0, early)
    _, turned = lax.optimization_barrier((upper, turned))
    swapped = lax.ppermute(turned, "ka", second_leg)
    imag, middle, turned, swapped, real_over = lax.optimization_barrier(
        (imag, middle, turned, swapped, real_over)
    )
    imag_over = lax.ppermute(imag, "ka", outside)
    lower = part(1, jnp.concatenate([middle, jnp.where(relayed, swapped, turned)]))
    within = jnp.concatenate([summed(upper), summed(lower)])
    real, imag, _ = lax.optimization_barrier((real, imag, lower))
    moved = scattered_rows([real, imag], gshift)
    products = second_plane(moved, imag_over, first_plane(moved, real_over))
    across = spread(products).reshape(slab_points, bands // pw_count, 2 * bands)

    result = reordered(order, wrapped.astype(jnp.int32).reshape(1), [within, across])
    result = result.reshape(slab_points, bands // pw_count, 2, bands)
    return jnp.transpose(result, (1, 0, 2, 3))


def solution(mesh):
    placed = (P("ka", None, "pw", None), P("ka"), P())
    return jax.shard_map(
        on_device, mesh=mesh, in_specs=placed, out_specs=P("pw", "ka", None, None), check_vma=False
    )
```

```python
import jax
import jax.numpy as jnp
from jax import lax
from jax.experimental import pallas as pl
from jax.experimental.pallas import tpu as pltpu
from jax.sharding import PartitionSpec as P

SHIFT_DEV = 2


def reordered(order, relayed, *pieces):
    sources = [source for piece in pieces for source in piece]
    count, _, bands = sources[0].shape
    rows = sum(piece[0].shape[1] for piece in pieces)
    shape, dtype = (count, rows, bands), sources[0].dtype

    def kernel(order, relayed, *refs):
        *given, result, held, read, written = refs

        def fetches(choice):
            at, first, copies = 0, 0, []
            for p, piece in enumerate(pieces):
                source = given[at + min(choice, len(piece) - 1)]
                height = piece[0].shape[1]
                copies += [
                    pltpu.make_async_copy(
                        source.at[order[i]], held.at[i, pl.ds(first, height)], read.at[p, i]
                    )
                    for i in range(count)
                ]
                at, first = at + len(piece), first + height
            return copies

        stores = [
            pltpu.make_async_copy(held.at[i], result.at[i], written.at[i]) for i in range(count)
        ]
        for choice in range(max(len(piece) for piece in pieces)):

            @pl.when(relayed[0] == choice)
            def _(choice=choice):
                copies = fetches(choice)
                for copy in copies:
                    copy.start()
                for i in range(count):
                    for copy in copies[i::count]:
                        copy.wait()
                    stores[i].start()

        for store in stores:
            store.wait()

    return pl.pallas_call(
        kernel,
        grid_spec=pltpu.PrefetchScalarGridSpec(
            num_scalar_prefetch=2,
            grid=(),
            in_specs=[pl.BlockSpec(memory_space=pltpu.HBM)] * len(sources),
            out_specs=pl.BlockSpec(memory_space=pltpu.HBM),
            scratch_shapes=[
                pltpu.VMEM(shape, dtype),
                pltpu.SemaphoreType.DMA((len(pieces), count)),
                pltpu.SemaphoreType.DMA((count,)),
            ],
        ),
        out_shape=jax.ShapeDtypeStruct(shape, dtype),
        compiler_params=pltpu.CompilerParams(vmem_limit_bytes=56 << 20),
        cost_estimate=pl.CostEstimate(
            flops=0, bytes_accessed=2 * count * rows * bands * dtype.itemsize, transcendentals=0
        ),
    )(order, relayed, *sources)


def scatter_rows_kernel(target_ref, real_ref, imag_ref, out_ref):
    sources, rows, bands = real_ref.shape
    height = out_ref.shape[2]
    first = pl.program_id(0) * height
    pair = 2
    wanted = first + lax.broadcasted_iota(jnp.int32, (height, pair * rows), 0)
    totals = [jnp.zeros((height, bands), jnp.float32) for _ in range(2)]
    for s in range(0, sources, pair):
        hot = (target_ref[:, s * rows : (s + pair) * rows] == wanted).astype(jnp.bfloat16)
        for c, plane in enumerate((real_ref, imag_ref)):
            block = plane[s : s + pair].reshape(pair * rows, bands)
            totals[c] += jnp.dot(hot, block, preferred_element_type=jnp.float32)
    for c in range(2):
        out_ref[c] = totals[c].T.astype(out_ref.dtype)


def scattered_rows(planes, target):
    sources, rows, bands = planes[0].shape
    total = sources * rows
    height = 256
    whole = pl.BlockSpec(planes[0].shape, lambda i: (0, 0, 0), pipeline_mode=pl.Buffered(1))
    return pl.pallas_call(
        scatter_rows_kernel,
        grid=(total // height,),
        in_specs=[pl.BlockSpec((1, total), lambda i: (0, 0)), whole, whole],
        out_specs=pl.BlockSpec((2, bands, height), lambda i: (0, 0, i)),
        out_shape=jax.ShapeDtypeStruct((2, bands, total), planes[0].dtype),
        compiler_params=pltpu.CompilerParams(vmem_limit_bytes=56 << 20),
        cost_estimate=pl.CostEstimate(
            flops=4 * total * total * bands, bytes_accessed=8 * planes[0].size, transcendentals=0
        ),
    )(target.reshape(1, total), *planes)


def ordered_planes_kernel(order, source, real, imag, held, read, written):
    count = real.shape[0]
    fetches, stores = [], []
    for c, result in enumerate((real, imag)):
        for i in range(count):
            fetches.append(
                pltpu.make_async_copy(source.at[order[i], c], held.at[c, i], read.at[c, i])
            )
            stores.append(pltpu.make_async_copy(held.at[c, i], result.at[i], written.at[c, i]))
    for copy in fetches:
        copy.start()
    for fetch, store in zip(fetches, stores):
        fetch.wait()
        store.start()
    for store in stores:
        store.wait()


def ordered_planes(source, order):
    count, parts, rows, bands = source.shape
    plane = jax.ShapeDtypeStruct((count, rows, bands), source.dtype)
    return pl.pallas_call(
        ordered_planes_kernel,
        grid_spec=pltpu.PrefetchScalarGridSpec(
            num_scalar_prefetch=1,
            grid=(),
            in_specs=[pl.BlockSpec(memory_space=pltpu.HBM)],
            out_specs=[pl.BlockSpec(memory_space=pltpu.HBM)] * 2,
            scratch_shapes=[
                pltpu.VMEM((parts, count, rows, bands), source.dtype),
                pltpu.SemaphoreType.DMA((parts, count)),
                pltpu.SemaphoreType.DMA((parts, count)),
            ],
        ),
        out_shape=[plane, plane],
        compiler_params=pltpu.CompilerParams(vmem_limit_bytes=56 << 20),
        cost_estimate=pl.CostEstimate(flops=0, bytes_accessed=4 * source.size, transcendentals=0),
    )(order, source)


def slab_kernel(own_of, own_ref, partner_ref, out_ref):
    own = [own_ref[0, c] for c in range(2)]
    partner = [partner_ref[0, d] for d in range(2)]

    def product(c, d):
        return lax.dot_general(
            own[c], partner[d], (((0,), (0,)), ((), ())), preferred_element_type=jnp.float32
        )

    groups, _, height, width = out_ref.shape
    bands = width // 2
    real = product(0, 0) + product(1, 1)
    imag = product(0, 1) - product(1, 0)
    out_ref[:, 0, :, :bands] = real.reshape(groups, height, bands)
    out_ref[:, 0, :, bands:] = imag.reshape(groups, height, bands)


def slab_products(coeffs, partner, own_of, groups):
    count, parts, rows, bands = partner.shape
    block = (1, parts, rows, bands)
    return pl.pallas_call(
        slab_kernel,
        grid_spec=pltpu.PrefetchScalarGridSpec(
            num_scalar_prefetch=1,
            grid=(count,),
            in_specs=[
                pl.BlockSpec(block, lambda j, own_of: (own_of[j], 0, 0, 0)),
                pl.BlockSpec(block, lambda j, own_of: (j, 0, 0, 0)),
            ],
            out_specs=pl.BlockSpec(
                (groups, 1, bands // groups, 2 * bands), lambda j, own_of: (0, j, 0, 0)
            ),
        ),
        out_shape=jax.ShapeDtypeStruct((groups, count, bands // groups, 2 * bands), jnp.float32),
        compiler_params=pltpu.CompilerParams(vmem_limit_bytes=56 << 20),
        cost_estimate=pl.CostEstimate(
            flops=8 * count * rows * bands * bands,
            bytes_accessed=4 * partner.size + 8 * count * bands * bands,
            transcendentals=0,
        ),
    )(own_of, coeffs, partner)


def plane_products(own_ref, partner_ref):
    sources, rows, bands = partner_ref.shape
    partner = partner_ref[...].reshape(sources * rows, bands)
    own = own_ref[...].reshape(-1, sources * rows)
    both = jnp.dot(own, partner, preferred_element_type=jnp.float32)
    return both[:bands], both[bands:]


def first_plane_kernel(own_ref, partner_ref, out_ref):
    @pl.when(pl.program_id(0) == 0)
    def _():
        out_ref[...] = jnp.zeros_like(out_ref)

    real, imag = plane_products(own_ref, partner_ref)
    out_ref[0] += real
    out_ref[1] -= imag


def second_plane_kernel(own_ref, partner_ref, first_ref, out_ref, acc_ref):
    step = pl.program_id(0)

    @pl.when(step == 0)
    def _():
        acc_ref[...] = first_ref[...]

    imag, real = plane_products(own_ref, partner_ref)
    acc_ref[0] += real
    acc_ref[1] += imag

    @pl.when(step == pl.num_programs(0) - 1)
    def _():
        bands = acc_ref.shape[1]
        for d in range(2):
            out_ref[:, d * bands : (d + 1) * bands] = acc_ref[d]


TAKE = 8


def pair_specs(own, partner):
    sources, rows, bands = partner.shape
    specs = [
        pl.BlockSpec((own.shape[0], bands, TAKE * rows), lambda i: (0, 0, i)),
        pl.BlockSpec((TAKE, rows, bands), lambda i: (i, 0, 0)),
    ]
    cost = pl.CostEstimate(
        flops=4 * sources * rows * bands * bands, bytes_accessed=6 * partner.size, transcendentals=0
    )
    return (sources // TAKE,), specs, cost


def first_plane(own, partner):
    grid, specs, cost = pair_specs(own, partner)
    bands = own.shape[1]
    return pl.pallas_call(
        first_plane_kernel,
        grid=grid,
        in_specs=specs,
        out_specs=pl.BlockSpec((2, bands, bands), lambda i: (0, 0, 0)),
        out_shape=jax.ShapeDtypeStruct((2, bands, bands), jnp.float32),
        compiler_params=pltpu.CompilerParams(vmem_limit_bytes=56 << 20),
        cost_estimate=cost,
    )(own, partner)


def second_plane(own, partner, first):
    grid, specs, cost = pair_specs(own, partner)
    bands = own.shape[1]
    return pl.pallas_call(
        second_plane_kernel,
        grid=grid,
        in_specs=specs + [pl.BlockSpec(first.shape, lambda i: (0, 0, 0))],
        out_specs=pl.BlockSpec((bands, 2 * bands), lambda i: (0, 0)),
        out_shape=jax.ShapeDtypeStruct((bands, 2 * bands), jnp.float32),
        scratch_shapes=[pltpu.VMEM(first.shape, jnp.float32)],
        compiler_params=pltpu.CompilerParams(vmem_limit_bytes=56 << 20),
        cost_estimate=cost,
    )(own, partner, first)


SIDES = 2


def on_device(coeffs, neighbour, gshift):
    slab_points, parts, rows, bands = coeffs.shape
    ka_count, pw_count = lax.axis_size("ka"), lax.axis_size("pw")
    wrapped = lax.axis_index("ka") >= ka_count - SHIFT_DEV
    side = lax.axis_index("pw") % SIDES
    points = lax.iota(jnp.int32, slab_points)

    def spread(block):
        return lax.all_to_all(block, "pw", split_axis=0, concat_axis=0, tiled=True)

    order = neighbour % slab_points
    own_of = jnp.sum(jnp.where(order[None, :] == points[:, None], points[None, :], 0), axis=1)
    inside = [(i + SHIFT_DEV, i) for i in range(ka_count - SHIFT_DEV)]
    outside = [((i + SHIFT_DEV) % ka_count, i) for i in range(ka_count - SHIFT_DEV, ka_count)]

    planes = ordered_planes(coeffs, jnp.where(wrapped, own_of, points))
    levels = pw_count // SIDES
    columns = [[z * SIDES + x for z in range(levels)] for x in range(SIDES)]
    swap = [(i, i + 1 - 2 * (i % SIDES)) for i in range(pw_count)]
    height = slab_points // 2
    def part(i, block):
        own = own_of[i * height : (i + 1) * height]
        return slab_products(coeffs, block, own, levels)

    def summed(block):
        block = lax.psum_scatter(
            block, "pw", scatter_dimension=0, axis_index_groups=columns, tiled=True
        ).reshape(height, SIDES, bands // pw_count, 2 * bands)
        keep = lax.dynamic_index_in_dim(block, side, 1, keepdims=False)
        give = lax.dynamic_index_in_dim(block, 1 - side, 1, keepdims=False)
        return keep + lax.ppermute(give, "pw", swap)

    early = lax.ppermute(coeffs[:height], "ka", inside)
    real = spread(planes[0])
    real, later, early, late = lax.optimization_barrier((real, planes[1], early, coeffs[height:]))
    imag = spread(later)
    late = lax.ppermute(late, "ka", inside)
    real_over = lax.ppermute(real, "ka", outside)
    upper = part(0, early)
    imag, _, late, real_over = lax.optimization_barrier((imag, upper, late, real_over))
    imag_over = lax.ppermute(imag, "ka", outside)
    lower = part(1, late)
    within = jnp.concatenate([summed(upper), summed(lower)])
    real, imag, _ = lax.optimization_barrier((real, imag, lower))
    moved = scattered_rows([real, imag], gshift)
    products = second_plane(moved, imag_over, first_plane(moved, real_over))
    across = spread(products).reshape(slab_points, bands // pw_count, 2 * bands)

    result = reordered(order, wrapped.astype(jnp.int32).reshape(1), [within, across])
    result = result.reshape(slab_points, bands // pw_count, 2, bands)
    return jnp.transpose(result, (1, 0, 2, 3))


def solution(mesh):
    placed = (P("ka", None, "pw", None), P("ka"), P())
    return jax.shard_map(
        on_device, mesh=mesh, in_specs=placed, out_specs=P("pw", "ka", None, None), check_vma=False
    )
```

```python
import jax
import jax.numpy as jnp
from jax import lax
from jax.experimental import pallas as pl
from jax.experimental.pallas import tpu as pltpu
from jax.sharding import PartitionSpec as P

SHIFT_DEV = 2


def reordered(order, relayed, *pieces):
    sources = [source for piece in pieces for source in piece]
    count, _, bands = sources[0].shape
    rows = sum(piece[0].shape[1] for piece in pieces)
    shape, dtype = (count, rows, bands), sources[0].dtype

    def kernel(order, relayed, *refs):
        *given, result, held, read, written = refs

        def fetches(choice):
            at, first, copies = 0, 0, []
            for p, piece in enumerate(pieces):
                source = given[at + min(choice, len(piece) - 1)]
                height = piece[0].shape[1]
                copies += [
                    pltpu.make_async_copy(
                        source.at[order[i]], held.at[i, pl.ds(first, height)], read.at[p, i]
                    )
                    for i in range(count)
                ]
                at, first = at + len(piece), first + height
            return copies

        stores = [
            pltpu.make_async_copy(held.at[i], result.at[i], written.at[i]) for i in range(count)
        ]
        for choice in range(max(len(piece) for piece in pieces)):

            @pl.when(relayed[0] == choice)
            def _(choice=choice):
                copies = fetches(choice)
                for copy in copies:
                    copy.start()
                for i in range(count):
                    for copy in copies[i::count]:
                        copy.wait()
                    stores[i].start()

        for store in stores:
            store.wait()

    return pl.pallas_call(
        kernel,
        grid_spec=pltpu.PrefetchScalarGridSpec(
            num_scalar_prefetch=2,
            grid=(),
            in_specs=[pl.BlockSpec(memory_space=pltpu.HBM)] * len(sources),
            out_specs=pl.BlockSpec(memory_space=pltpu.HBM),
            scratch_shapes=[
                pltpu.VMEM(shape, dtype),
                pltpu.SemaphoreType.DMA((len(pieces), count)),
                pltpu.SemaphoreType.DMA((count,)),
            ],
        ),
        out_shape=jax.ShapeDtypeStruct(shape, dtype),
        compiler_params=pltpu.CompilerParams(vmem_limit_bytes=56 << 20),
        cost_estimate=pl.CostEstimate(
            flops=0, bytes_accessed=2 * count * rows * bands * dtype.itemsize, transcendentals=0
        ),
    )(order, relayed, *sources)


def scatter_rows_kernel(target_ref, real_ref, imag_ref, out_ref):
    sources, rows, bands = real_ref.shape
    height = out_ref.shape[2]
    first = pl.program_id(0) * height
    pair = 2
    wanted = first + lax.broadcasted_iota(jnp.int32, (height, pair * rows), 0)
    totals = [jnp.zeros((height, bands), jnp.float32) for _ in range(2)]
    for s in range(0, sources, pair):
        hot = (target_ref[:, s * rows : (s + pair) * rows] == wanted).astype(jnp.bfloat16)
        for c, plane in enumerate((real_ref, imag_ref)):
            block = plane[s : s + pair].reshape(pair * rows, bands)
            totals[c] += jnp.dot(hot, block, preferred_element_type=jnp.float32)
    for c in range(2):
        out_ref[c] = totals[c].T.astype(out_ref.dtype)


def scattered_rows(planes, target):
    sources, rows, bands = planes[0].shape
    total = sources * rows
    height = 256
    whole = pl.BlockSpec(planes[0].shape, lambda i: (0, 0, 0), pipeline_mode=pl.Buffered(1))
    return pl.pallas_call(
        scatter_rows_kernel,
        grid=(total // height,),
        in_specs=[pl.BlockSpec((1, total), lambda i: (0, 0)), whole, whole],
        out_specs=pl.BlockSpec((2, bands, height), lambda i: (0, 0, i)),
        out_shape=jax.ShapeDtypeStruct((2, bands, total), planes[0].dtype),
        compiler_params=pltpu.CompilerParams(vmem_limit_bytes=56 << 20),
        cost_estimate=pl.CostEstimate(
            flops=4 * total * total * bands, bytes_accessed=8 * planes[0].size, transcendentals=0
        ),
    )(target.reshape(1, total), *planes)


def ordered_planes_kernel(order, source, real, imag, held, read, written):
    count = real.shape[0]
    fetches, stores = [], []
    for c, result in enumerate((real, imag)):
        for i in range(count):
            fetches.append(
                pltpu.make_async_copy(source.at[order[i], c], held.at[c, i], read.at[c, i])
            )
            stores.append(pltpu.make_async_copy(held.at[c, i], result.at[i], written.at[c, i]))
    for copy in fetches:
        copy.start()
    for fetch, store in zip(fetches, stores):
        fetch.wait()
        store.start()
    for store in stores:
        store.wait()


def ordered_planes(source, order):
    count, parts, rows, bands = source.shape
    plane = jax.ShapeDtypeStruct((count, rows, bands), source.dtype)
    return pl.pallas_call(
        ordered_planes_kernel,
        grid_spec=pltpu.PrefetchScalarGridSpec(
            num_scalar_prefetch=1,
            grid=(),
            in_specs=[pl.BlockSpec(memory_space=pltpu.HBM)],
            out_specs=[pl.BlockSpec(memory_space=pltpu.HBM)] * 2,
            scratch_shapes=[
                pltpu.VMEM((parts, count, rows, bands), source.dtype),
                pltpu.SemaphoreType.DMA((parts, count)),
                pltpu.SemaphoreType.DMA((parts, count)),
            ],
        ),
        out_shape=[plane, plane],
        compiler_params=pltpu.CompilerParams(vmem_limit_bytes=56 << 20),
        cost_estimate=pl.CostEstimate(flops=0, bytes_accessed=4 * source.size, transcendentals=0),
    )(order, source)


def slab_kernel(own_of, own_ref, partner_ref, out_ref):
    own = [own_ref[0, c] for c in range(2)]
    partner = [partner_ref[0, d] for d in range(2)]

    def product(c, d):
        return lax.dot_general(
            own[c], partner[d], (((0,), (0,)), ((), ())), preferred_element_type=jnp.float32
        )

    groups, _, height, width = out_ref.shape
    bands = width // 2
    real = product(0, 0) + product(1, 1)
    imag = product(0, 1) - product(1, 0)
    out_ref[:, 0, :, :bands] = real.reshape(groups, height, bands)
    out_ref[:, 0, :, bands:] = imag.reshape(groups, height, bands)


def slab_products(coeffs, partner, own_of, groups):
    count, parts, rows, bands = partner.shape
    block = (1, parts, rows, bands)
    return pl.pallas_call(
        slab_kernel,
        grid_spec=pltpu.PrefetchScalarGridSpec(
            num_scalar_prefetch=1,
            grid=(count,),
            in_specs=[
                pl.BlockSpec(block, lambda j, own_of: (own_of[j], 0, 0, 0)),
                pl.BlockSpec(block, lambda j, own_of: (j, 0, 0, 0)),
            ],
            out_specs=pl.BlockSpec(
                (groups, 1, bands // groups, 2 * bands), lambda j, own_of: (0, j, 0, 0)
            ),
        ),
        out_shape=jax.ShapeDtypeStruct((groups, count, bands // groups, 2 * bands), jnp.float32),
        compiler_params=pltpu.CompilerParams(vmem_limit_bytes=56 << 20),
        cost_estimate=pl.CostEstimate(
            flops=8 * count * rows * bands * bands,
            bytes_accessed=4 * partner.size + 8 * count * bands * bands,
            transcendentals=0,
        ),
    )(own_of, coeffs, partner)


def plane_products(own_ref, partner_ref):
    sources, rows, bands = partner_ref.shape
    partner = partner_ref[...].reshape(sources * rows, bands)
    own = own_ref[...].reshape(-1, sources * rows)
    both = jnp.dot(own, partner, preferred_element_type=jnp.float32)
    return both[:bands], both[bands:]


def first_plane_kernel(own_ref, partner_ref, out_ref):
    @pl.when(pl.program_id(0) == 0)
    def _():
        out_ref[...] = jnp.zeros_like(out_ref)

    real, imag = plane_products(own_ref, partner_ref)
    out_ref[0] += real
    out_ref[1] -= imag


def second_plane_kernel(own_ref, partner_ref, first_ref, out_ref, acc_ref):
    step = pl.program_id(0)

    @pl.when(step == 0)
    def _():
        acc_ref[...] = first_ref[...]

    imag, real = plane_products(own_ref, partner_ref)
    acc_ref[0] += real
    acc_ref[1] += imag

    @pl.when(step == pl.num_programs(0) - 1)
    def _():
        bands = acc_ref.shape[1]
        for d in range(2):
            out_ref[:, d * bands : (d + 1) * bands] = acc_ref[d]


TAKE = 8


def pair_specs(own, partner):
    sources, rows, bands = partner.shape
    specs = [
        pl.BlockSpec((own.shape[0], bands, TAKE * rows), lambda i: (0, 0, i)),
        pl.BlockSpec((TAKE, rows, bands), lambda i: (i, 0, 0)),
    ]
    cost = pl.CostEstimate(
        flops=4 * sources * rows * bands * bands, bytes_accessed=6 * partner.size, transcendentals=0
    )
    return (sources // TAKE,), specs, cost


def first_plane(own, partner):
    grid, specs, cost = pair_specs(own, partner)
    bands = own.shape[1]
    return pl.pallas_call(
        first_plane_kernel,
        grid=grid,
        in_specs=specs,
        out_specs=pl.BlockSpec((2, bands, bands), lambda i: (0, 0, 0)),
        out_shape=jax.ShapeDtypeStruct((2, bands, bands), jnp.float32),
        compiler_params=pltpu.CompilerParams(vmem_limit_bytes=56 << 20),
        cost_estimate=cost,
    )(own, partner)


def second_plane(own, partner, first):
    grid, specs, cost = pair_specs(own, partner)
    bands = own.shape[1]
    return pl.pallas_call(
        second_plane_kernel,
        grid=grid,
        in_specs=specs + [pl.BlockSpec(first.shape, lambda i: (0, 0, 0))],
        out_specs=pl.BlockSpec((bands, 2 * bands), lambda i: (0, 0)),
        out_shape=jax.ShapeDtypeStruct((bands, 2 * bands), jnp.float32),
        scratch_shapes=[pltpu.VMEM(first.shape, jnp.float32)],
        compiler_params=pltpu.CompilerParams(vmem_limit_bytes=56 << 20),
        cost_estimate=cost,
    )(own, partner, first)


SIDES = 2


def on_device(coeffs, neighbour, gshift):
    slab_points, parts, rows, bands = coeffs.shape
    ka_count, pw_count = lax.axis_size("ka"), lax.axis_size("pw")
    wrapped = lax.axis_index("ka") >= ka_count - SHIFT_DEV
    side = lax.axis_index("pw") % SIDES
    points = lax.iota(jnp.int32, slab_points)

    def spread(block):
        return lax.all_to_all(block, "pw", split_axis=0, concat_axis=0, tiled=True)

    order = neighbour % slab_points
    own_of = jnp.sum(jnp.where(order[None, :] == points[:, None], points[None, :], 0), axis=1)
    inside = [(i + SHIFT_DEV, i) for i in range(ka_count - SHIFT_DEV)]
    outside = [((i + SHIFT_DEV) % ka_count, i) for i in range(ka_count - SHIFT_DEV, ka_count)]

    planes = ordered_planes(coeffs, jnp.where(wrapped, own_of, points))
    levels = pw_count // SIDES
    columns = [[z * SIDES + x for z in range(levels)] for x in range(SIDES)]
    swap = [(i, i + 1 - 2 * (i % SIDES)) for i in range(pw_count)]
    height = slab_points // 2
    here = lax.axis_index("ka")
    engaged = wrapped | (here < SHIFT_DEV)

    def spread_there(block):
        return lax.cond(engaged, spread, lambda block: block, block)

    def part(i, block):
        own = own_of[i * height : (i + 1) * height]
        return slab_products(coeffs, block, own, levels)

    def summed_over_z(block):
        return lax.psum_scatter(
            block, "pw", scatter_dimension=0, axis_index_groups=columns, tiled=True
        )

    def summed(block):
        block = block.reshape(height, SIDES, bands // pw_count, 2 * bands)
        keep = lax.dynamic_index_in_dim(block, side, 1, keepdims=False)
        give = lax.dynamic_index_in_dim(block, 1 - side, 1, keepdims=False)
        return keep + lax.ppermute(give, "pw", swap)

    early = lax.ppermute(coeffs[:height], "ka", inside)
    real = spread_there(planes[0])
    real, later, early, late = lax.optimization_barrier((real, planes[1], early, coeffs[height:]))
    imag = spread_there(later)
    late = lax.ppermute(late, "ka", inside)
    real_over = lax.ppermute(real, "ka", outside)
    upper = part(0, early)
    imag, _, late, real_over = lax.optimization_barrier((imag, upper, late, real_over))
    imag_over = lax.ppermute(imag, "ka", outside)
    lower = part(1, late)
    sums = [summed_over_z(upper), summed_over_z(lower)]
    real, imag, _ = lax.optimization_barrier((real, imag, lower))
    rows_all = gshift.shape[0]
    moved = lax.cond(
        wrapped,
        lambda real, imag: scattered_rows([real, imag], gshift),
        lambda real, imag: jnp.zeros((2, bands, rows_all), real.dtype),
        real,
        imag,
    )

    moved, *sums = lax.optimization_barrier((moved, *sums))
    within = jnp.concatenate([summed(block) for block in sums])

    def finished(moved, real, imag):
        return spread(second_plane(moved, imag, first_plane(moved, real)))

    def empty(moved, real, imag):
        return jnp.zeros((bands, 2 * bands), jnp.float32)

    across = lax.cond(wrapped, finished, empty, moved, real_over, imag_over)
    across = across.reshape(slab_points, bands // pw_count, 2 * bands)

    result = reordered(order, wrapped.astype(jnp.int32).reshape(1), [within, across])
    result = result.reshape(slab_points, bands // pw_count, 2, bands)
    return jnp.transpose(result, (1, 0, 2, 3))


def solution(mesh):
    placed = (P("ka", None, "pw", None), P("ka"), P())
    return jax.shard_map(
        on_device, mesh=mesh, in_specs=placed, out_specs=P("pw", "ka", None, None), check_vma=False
    )
```

```python
import jax
import jax.numpy as jnp
from jax import lax
from jax.experimental import pallas as pl
from jax.experimental.pallas import tpu as pltpu
from jax.sharding import PartitionSpec as P

SHIFT_DEV = 2


def reordered(order, relayed, *pieces):
    sources = [source for piece in pieces for source in piece]
    count, _, bands = sources[0].shape
    rows = sum(piece[0].shape[1] for piece in pieces)
    shape, dtype = (count, rows, bands), sources[0].dtype

    def kernel(order, relayed, *refs):
        *given, result, held, read, written = refs

        def fetches(choice):
            at, first, copies = 0, 0, []
            for p, piece in enumerate(pieces):
                source = given[at + min(choice, len(piece) - 1)]
                height = piece[0].shape[1]
                copies += [
                    pltpu.make_async_copy(
                        source.at[order[i]], held.at[i, pl.ds(first, height)], read.at[p, i]
                    )
                    for i in range(count)
                ]
                at, first = at + len(piece), first + height
            return copies

        stores = [
            pltpu.make_async_copy(held.at[i], result.at[i], written.at[i]) for i in range(count)
        ]
        for choice in range(max(len(piece) for piece in pieces)):

            @pl.when(relayed[0] == choice)
            def _(choice=choice):
                copies = fetches(choice)
                for copy in copies:
                    copy.start()
                for i in range(count):
                    for copy in copies[i::count]:
                        copy.wait()
                    stores[i].start()

        for store in stores:
            store.wait()

    return pl.pallas_call(
        kernel,
        grid_spec=pltpu.PrefetchScalarGridSpec(
            num_scalar_prefetch=2,
            grid=(),
            in_specs=[pl.BlockSpec(memory_space=pltpu.HBM)] * len(sources),
            out_specs=pl.BlockSpec(memory_space=pltpu.HBM),
            scratch_shapes=[
                pltpu.VMEM(shape, dtype),
                pltpu.SemaphoreType.DMA((len(pieces), count)),
                pltpu.SemaphoreType.DMA((count,)),
            ],
        ),
        out_shape=jax.ShapeDtypeStruct(shape, dtype),
        compiler_params=pltpu.CompilerParams(vmem_limit_bytes=56 << 20),
        cost_estimate=pl.CostEstimate(
            flops=0, bytes_accessed=2 * count * rows * bands * dtype.itemsize, transcendentals=0
        ),
    )(order, relayed, *sources)


def scatter_rows_kernel(target_ref, real_ref, imag_ref, out_ref):
    sources, rows, bands = real_ref.shape
    height = out_ref.shape[2]
    first = pl.program_id(0) * height
    pair = 2
    wanted = first + lax.broadcasted_iota(jnp.int32, (height, pair * rows), 0)
    totals = [jnp.zeros((height, bands), jnp.float32) for _ in range(2)]
    for s in range(0, sources, pair):
        hot = (target_ref[:, s * rows : (s + pair) * rows] == wanted).astype(jnp.bfloat16)
        for c, plane in enumerate((real_ref, imag_ref)):
            block = plane[s : s + pair].reshape(pair * rows, bands)
            totals[c] += jnp.dot(hot, block, preferred_element_type=jnp.float32)
    for c in range(2):
        out_ref[c] = totals[c].T.astype(out_ref.dtype)


def scattered_rows(planes, target):
    sources, rows, bands = planes[0].shape
    total = sources * rows
    height = 256
    whole = pl.BlockSpec(planes[0].shape, lambda i: (0, 0, 0), pipeline_mode=pl.Buffered(1))
    return pl.pallas_call(
        scatter_rows_kernel,
        grid=(total // height,),
        in_specs=[pl.BlockSpec((1, total), lambda i: (0, 0)), whole, whole],
        out_specs=pl.BlockSpec((2, bands, height), lambda i: (0, 0, i)),
        out_shape=jax.ShapeDtypeStruct((2, bands, total), planes[0].dtype),
        compiler_params=pltpu.CompilerParams(vmem_limit_bytes=56 << 20),
        cost_estimate=pl.CostEstimate(
            flops=4 * total * total * bands, bytes_accessed=8 * planes[0].size, transcendentals=0
        ),
    )(target.reshape(1, total), *planes)


def ordered_planes_kernel(order, source, real, imag, held, read, written):
    count = real.shape[0]
    fetches, stores = [], []
    for c, result in enumerate((real, imag)):
        for i in range(count):
            fetches.append(
                pltpu.make_async_copy(source.at[order[i], c], held.at[c, i], read.at[c, i])
            )
            stores.append(pltpu.make_async_copy(held.at[c, i], result.at[i], written.at[c, i]))
    for copy in fetches:
        copy.start()
    for fetch, store in zip(fetches, stores):
        fetch.wait()
        store.start()
    for store in stores:
        store.wait()


def ordered_planes(source, order):
    count, parts, rows, bands = source.shape
    plane = jax.ShapeDtypeStruct((count, rows, bands), source.dtype)
    return pl.pallas_call(
        ordered_planes_kernel,
        grid_spec=pltpu.PrefetchScalarGridSpec(
            num_scalar_prefetch=1,
            grid=(),
            in_specs=[pl.BlockSpec(memory_space=pltpu.HBM)],
            out_specs=[pl.BlockSpec(memory_space=pltpu.HBM)] * 2,
            scratch_shapes=[
                pltpu.VMEM((parts, count, rows, bands), source.dtype),
                pltpu.SemaphoreType.DMA((parts, count)),
                pltpu.SemaphoreType.DMA((parts, count)),
            ],
        ),
        out_shape=[plane, plane],
        compiler_params=pltpu.CompilerParams(vmem_limit_bytes=56 << 20),
        cost_estimate=pl.CostEstimate(flops=0, bytes_accessed=4 * source.size, transcendentals=0),
    )(order, source)


def slab_kernel(own_of, own_ref, partner_ref, out_ref):
    own = [own_ref[0, c] for c in range(2)]
    partner = [partner_ref[0, d] for d in range(2)]

    def product(c, d):
        return lax.dot_general(
            own[c], partner[d], (((0,), (0,)), ((), ())), preferred_element_type=jnp.float32
        )

    groups, _, height, width = out_ref.shape
    bands = width // 2
    real = product(0, 0) + product(1, 1)
    imag = product(0, 1) - product(1, 0)
    out_ref[:, 0, :, :bands] = real.reshape(groups, height, bands)
    out_ref[:, 0, :, bands:] = imag.reshape(groups, height, bands)


def slab_products(coeffs, partner, own_of, groups):
    count, parts, rows, bands = partner.shape
    block = (1, parts, rows, bands)
    return pl.pallas_call(
        slab_kernel,
        grid_spec=pltpu.PrefetchScalarGridSpec(
            num_scalar_prefetch=1,
            grid=(count,),
            in_specs=[
                pl.BlockSpec(block, lambda j, own_of: (own_of[j], 0, 0, 0)),
                pl.BlockSpec(block, lambda j, own_of: (j, 0, 0, 0)),
            ],
            out_specs=pl.BlockSpec(
                (groups, 1, bands // groups, 2 * bands), lambda j, own_of: (0, j, 0, 0)
            ),
        ),
        out_shape=jax.ShapeDtypeStruct((groups, count, bands // groups, 2 * bands), jnp.float32),
        compiler_params=pltpu.CompilerParams(vmem_limit_bytes=56 << 20),
        cost_estimate=pl.CostEstimate(
            flops=8 * count * rows * bands * bands,
            bytes_accessed=4 * partner.size + 8 * count * bands * bands,
            transcendentals=0,
        ),
    )(own_of, coeffs, partner)


def plane_products(own_ref, partner_ref):
    sources, rows, bands = partner_ref.shape
    partner = partner_ref[...].reshape(sources * rows, bands)
    own = own_ref[...].reshape(-1, sources * rows)
    both = jnp.dot(own, partner, preferred_element_type=jnp.float32)
    return both[:bands], both[bands:]


def first_plane_kernel(own_ref, partner_ref, out_ref):
    @pl.when(pl.program_id(0) == 0)
    def _():
        out_ref[...] = jnp.zeros_like(out_ref)

    real, imag = plane_products(own_ref, partner_ref)
    out_ref[0] += real
    out_ref[1] -= imag


def second_plane_kernel(own_ref, partner_ref, first_ref, out_ref, acc_ref):
    step = pl.program_id(0)

    @pl.when(step == 0)
    def _():
        acc_ref[...] = first_ref[...]

    imag, real = plane_products(own_ref, partner_ref)
    acc_ref[0] += real
    acc_ref[1] += imag

    @pl.when(step == pl.num_programs(0) - 1)
    def _():
        bands = acc_ref.shape[1]
        for d in range(2):
            out_ref[:, d * bands : (d + 1) * bands] = acc_ref[d]


TAKE = 8


def pair_specs(own, partner):
    sources, rows, bands = partner.shape
    specs = [
        pl.BlockSpec((own.shape[0], bands, TAKE * rows), lambda i: (0, 0, i)),
        pl.BlockSpec((TAKE, rows, bands), lambda i: (i, 0, 0)),
    ]
    cost = pl.CostEstimate(
        flops=4 * sources * rows * bands * bands, bytes_accessed=6 * partner.size, transcendentals=0
    )
    return (sources // TAKE,), specs, cost


def first_plane(own, partner):
    grid, specs, cost = pair_specs(own, partner)
    bands = own.shape[1]
    return pl.pallas_call(
        first_plane_kernel,
        grid=grid,
        in_specs=specs,
        out_specs=pl.BlockSpec((2, bands, bands), lambda i: (0, 0, 0)),
        out_shape=jax.ShapeDtypeStruct((2, bands, bands), jnp.float32),
        compiler_params=pltpu.CompilerParams(vmem_limit_bytes=56 << 20),
        cost_estimate=cost,
    )(own, partner)


def second_plane(own, partner, first):
    grid, specs, cost = pair_specs(own, partner)
    bands = own.shape[1]
    return pl.pallas_call(
        second_plane_kernel,
        grid=grid,
        in_specs=specs + [pl.BlockSpec(first.shape, lambda i: (0, 0, 0))],
        out_specs=pl.BlockSpec((bands, 2 * bands), lambda i: (0, 0)),
        out_shape=jax.ShapeDtypeStruct((bands, 2 * bands), jnp.float32),
        scratch_shapes=[pltpu.VMEM(first.shape, jnp.float32)],
        compiler_params=pltpu.CompilerParams(vmem_limit_bytes=56 << 20),
        cost_estimate=cost,
    )(own, partner, first)


SIDES = 2


def on_device(coeffs, neighbour, gshift):
    slab_points, parts, rows, bands = coeffs.shape
    ka_count, pw_count = lax.axis_size("ka"), lax.axis_size("pw")
    wrapped = lax.axis_index("ka") >= ka_count - SHIFT_DEV
    side = lax.axis_index("pw") % SIDES
    points = lax.iota(jnp.int32, slab_points)

    def spread(block):
        return lax.all_to_all(block, "pw", split_axis=0, concat_axis=0, tiled=True)

    order = neighbour % slab_points
    own_of = jnp.sum(jnp.where(order[None, :] == points[:, None], points[None, :], 0), axis=1)
    inside = [(i + SHIFT_DEV, i) for i in range(ka_count - SHIFT_DEV)]
    outside = [((i + SHIFT_DEV) % ka_count, i) for i in range(ka_count - SHIFT_DEV, ka_count)]

    planes = ordered_planes(coeffs, jnp.where(wrapped, own_of, points))
    levels = pw_count // SIDES
    columns = [[z * SIDES + x for z in range(levels)] for x in range(SIDES)]
    swap = [(i, i + 1 - 2 * (i % SIDES)) for i in range(pw_count)]
    height = slab_points // 2
    here = lax.axis_index("ka")
    engaged = wrapped | (here < SHIFT_DEV)

    def spread_there(block):
        return lax.cond(engaged, spread, lambda block: block, block)

    def part(i, block):
        own = own_of[i * height : (i + 1) * height]
        return slab_products(coeffs, block, own, levels)

    def summed_over_z(block):
        return lax.psum_scatter(
            block, "pw", scatter_dimension=0, axis_index_groups=columns, tiled=True
        )

    def summed(block):
        block = block.reshape(height, SIDES, bands // pw_count, 2 * bands)
        keep = lax.dynamic_index_in_dim(block, side, 1, keepdims=False)
        give = lax.dynamic_index_in_dim(block, 1 - side, 1, keepdims=False)
        return keep + lax.ppermute(give, "pw", swap)

    early = lax.ppermute(coeffs[:height], "ka", inside)
    real = spread_there(planes[0])
    real, later, early, late = lax.optimization_barrier((real, planes[1], early, coeffs[height:]))
    imag = spread_there(later)
    late = lax.ppermute(late, "ka", inside)
    real_over = lax.ppermute(real, "ka", outside)
    imag, early, late, real_over = lax.optimization_barrier((imag, early, late, real_over))
    imag_over = lax.ppermute(imag, "ka", outside)
    upper = part(0, early)
    _, late = lax.optimization_barrier((upper, late))
    lower = part(1, late)
    sums = [summed_over_z(upper), summed_over_z(lower)]
    real, imag, _ = lax.optimization_barrier((real, imag, lower))
    rows_all = gshift.shape[0]
    moved = lax.cond(
        wrapped,
        lambda real, imag: scattered_rows([real, imag], gshift),
        lambda real, imag: jnp.zeros((2, bands, rows_all), real.dtype),
        real,
        imag,
    )

    moved, *sums = lax.optimization_barrier((moved, *sums))
    within = jnp.concatenate([summed(block) for block in sums])

    def finished(moved, real, imag):
        return spread(second_plane(moved, imag, first_plane(moved, real)))

    def empty(moved, real, imag):
        return jnp.zeros((bands, 2 * bands), jnp.float32)

    across = lax.cond(wrapped, finished, empty, moved, real_over, imag_over)
    across = across.reshape(slab_points, bands // pw_count, 2 * bands)

    result = reordered(order, wrapped.astype(jnp.int32).reshape(1), [within, across])
    result = result.reshape(slab_points, bands // pw_count, 2, bands)
    return jnp.transpose(result, (1, 0, 2, 3))


def solution(mesh):
    placed = (P("ka", None, "pw", None), P("ka"), P())
    return jax.shard_map(
        on_device, mesh=mesh, in_specs=placed, out_specs=P("pw", "ka", None, None), check_vma=False
    )
```

```python
import jax
import jax.numpy as jnp
from jax import lax
from jax.experimental import pallas as pl
from jax.experimental.pallas import tpu as pltpu
from jax.sharding import PartitionSpec as P

SHIFT_DEV = 2


def reordered(order, relayed, *pieces):
    sources = [source for piece in pieces for source in piece]
    count, _, bands = sources[0].shape
    rows = sum(piece[0].shape[1] for piece in pieces)
    shape, dtype = (count, rows, bands), sources[0].dtype

    def kernel(order, relayed, *refs):
        *given, result, held, read, written = refs

        def fetches(choice):
            at, first, copies = 0, 0, []
            for p, piece in enumerate(pieces):
                source = given[at + min(choice, len(piece) - 1)]
                height = piece[0].shape[1]
                copies += [
                    pltpu.make_async_copy(
                        source.at[order[i]], held.at[i, pl.ds(first, height)], read.at[p, i]
                    )
                    for i in range(count)
                ]
                at, first = at + len(piece), first + height
            return copies

        stores = [
            pltpu.make_async_copy(held.at[i], result.at[i], written.at[i]) for i in range(count)
        ]
        for choice in range(max(len(piece) for piece in pieces)):

            @pl.when(relayed[0] == choice)
            def _(choice=choice):
                copies = fetches(choice)
                for copy in copies:
                    copy.start()
                for i in range(count):
                    for copy in copies[i::count]:
                        copy.wait()
                    stores[i].start()

        for store in stores:
            store.wait()

    return pl.pallas_call(
        kernel,
        grid_spec=pltpu.PrefetchScalarGridSpec(
            num_scalar_prefetch=2,
            grid=(),
            in_specs=[pl.BlockSpec(memory_space=pltpu.HBM)] * len(sources),
            out_specs=pl.BlockSpec(memory_space=pltpu.HBM),
            scratch_shapes=[
                pltpu.VMEM(shape, dtype),
                pltpu.SemaphoreType.DMA((len(pieces), count)),
                pltpu.SemaphoreType.DMA((count,)),
            ],
        ),
        out_shape=jax.ShapeDtypeStruct(shape, dtype),
        compiler_params=pltpu.CompilerParams(vmem_limit_bytes=56 << 20),
        cost_estimate=pl.CostEstimate(
            flops=0, bytes_accessed=4 * count * rows * bands, transcendentals=0
        ),
    )(order, relayed, *sources)


def scatter_rows_kernel(target_ref, own_ref, out_ref):
    sources, parts, rows, bands = own_ref.shape
    height = out_ref.shape[2]
    first = pl.program_id(0) * height
    pair = 2
    wanted = first + lax.broadcasted_iota(jnp.int32, (height, pair * rows), 0)
    totals = [jnp.zeros((height, bands), jnp.float32) for _ in range(parts)]
    for s in range(0, sources, pair):
        hot = (target_ref[:, s * rows : (s + pair) * rows] == wanted).astype(jnp.bfloat16)
        for c in range(parts):
            block = own_ref[s : s + pair, c].reshape(pair * rows, bands)
            totals[c] += jnp.dot(hot, block, preferred_element_type=jnp.float32)
    for c in range(parts):
        out_ref[c] = totals[c].T.astype(out_ref.dtype)


def scattered_rows(own, target):
    sources, parts, rows, bands = own.shape
    total = sources * rows
    height = 256
    return pl.pallas_call(
        scatter_rows_kernel,
        grid=(total // height,),
        in_specs=[
            pl.BlockSpec((1, total), lambda i: (0, 0)),
            pl.BlockSpec(own.shape, lambda i: (0, 0, 0, 0), pipeline_mode=pl.Buffered(1)),
        ],
        out_specs=pl.BlockSpec((parts, bands, height), lambda i: (0, 0, i)),
        out_shape=jax.ShapeDtypeStruct((parts, bands, total), own.dtype),
        compiler_params=pltpu.CompilerParams(vmem_limit_bytes=56 << 20),
        cost_estimate=pl.CostEstimate(
            flops=2 * total * total * parts * bands, bytes_accessed=4 * own.size, transcendentals=0
        ),
    )(target.reshape(1, total), own)


def plane_products(own_ref, partner_ref):
    sources, rows, bands = partner_ref.shape
    partner = partner_ref[...].reshape(sources * rows, bands)
    own = own_ref[...].reshape(-1, sources * rows)
    both = jnp.dot(own, partner, preferred_element_type=jnp.float32)
    return both[:bands], both[bands:]


def first_plane_kernel(own_ref, partner_ref, out_ref):
    @pl.when(pl.program_id(0) == 0)
    def _():
        out_ref[...] = jnp.zeros_like(out_ref)

    real, imag = plane_products(own_ref, partner_ref)
    out_ref[0] += real
    out_ref[1] -= imag


def second_plane_kernel(own_ref, partner_ref, first_ref, out_ref, acc_ref):
    step = pl.program_id(0)

    @pl.when(step == 0)
    def _():
        acc_ref[...] = first_ref[...]

    imag, real = plane_products(own_ref, partner_ref)
    acc_ref[0] += real
    acc_ref[1] += imag

    @pl.when(step == pl.num_programs(0) - 1)
    def _():
        bands = acc_ref.shape[1]
        for d in range(2):
            out_ref[:, d * bands : (d + 1) * bands] = acc_ref[d]


TAKE = 8


def pair_specs(own, partner):
    sources, rows, bands = partner.shape
    specs = [
        pl.BlockSpec((own.shape[0], bands, TAKE * rows), lambda i: (0, 0, i)),
        pl.BlockSpec((TAKE, rows, bands), lambda i: (i, 0, 0)),
    ]
    cost = pl.CostEstimate(
        flops=4 * sources * rows * bands * bands, bytes_accessed=6 * partner.size, transcendentals=0
    )
    return (sources // TAKE,), specs, cost


def first_plane(own, partner):
    grid, specs, cost = pair_specs(own, partner)
    bands = own.shape[1]
    return pl.pallas_call(
        first_plane_kernel,
        grid=grid,
        in_specs=specs,
        out_specs=pl.BlockSpec((2, bands, bands), lambda i: (0, 0, 0)),
        out_shape=jax.ShapeDtypeStruct((2, bands, bands), jnp.float32),
        compiler_params=pltpu.CompilerParams(vmem_limit_bytes=24 << 20),
        cost_estimate=cost,
    )(own, partner)


def second_plane(own, partner, first):
    grid, specs, cost = pair_specs(own, partner)
    bands = own.shape[1]
    return pl.pallas_call(
        second_plane_kernel,
        grid=grid,
        in_specs=specs + [pl.BlockSpec(first.shape, lambda i: (0, 0, 0))],
        out_specs=pl.BlockSpec((bands, 2 * bands), lambda i: (0, 0)),
        out_shape=jax.ShapeDtypeStruct((bands, 2 * bands), jnp.float32),
        scratch_shapes=[pltpu.VMEM(first.shape, jnp.float32)],
        compiler_params=pltpu.CompilerParams(vmem_limit_bytes=24 << 20),
        cost_estimate=cost,
    )(own, partner, first)


def on_device(coeffs, neighbour, gshift):
    slab_points, parts, rows, bands = coeffs.shape
    ka_count = lax.axis_size("ka")
    here = lax.axis_index("ka")
    wrapped = here >= ka_count - SHIFT_DEV
    half = ka_count // 2
    crosses = here % half >= half - SHIFT_DEV

    def spread(block):
        return lax.all_to_all(block, "pw", split_axis=0, concat_axis=0, tiled=True)

    order = neighbour % slab_points
    own = spread(coeffs)
    straight = [((i + SHIFT_DEV) % ka_count, i) for i in range(ka_count)]
    around = [(i // half * half + (i + SHIFT_DEV) % half, i) for i in range(ka_count)]
    swap = [((i + half) % ka_count, i) for i in range(ka_count) if i % half >= half - SHIFT_DEV]
    cut = rows // 2
    direct = lax.ppermute(coeffs[:, 0], "ka", straight)
    turned = lax.ppermute(coeffs[:, 1, cut:], "ka", around)
    later = lax.ppermute(coeffs[:, 1, :cut], "ka", straight)
    waiting = reordered(order, jnp.zeros((1,), jnp.int32), [direct])
    own, waiting, turned = lax.optimization_barrier((own, waiting, turned))
    swapped = lax.ppermute(turned, "ka", swap)
    real = spread(waiting)
    target = jnp.where(wrapped, gshift, lax.iota(jnp.int32, gshift.shape[0]))
    moved = pltpu.with_memory_space_constraint(scattered_rows(own, target), pltpu.HBM)
    moved, swapped, later = lax.optimization_barrier((moved, swapped, later))
    waiting = reordered(order, crosses.astype(jnp.int32).reshape(1), [later], [turned, swapped])
    real, waiting = lax.optimization_barrier((real, waiting))
    imag = spread(waiting)
    first = pltpu.with_memory_space_constraint(first_plane(moved, real), pltpu.HBM)
    products = second_plane(moved, imag, first)
    products = spread(products).reshape(slab_points, bands // slab_points, 2, bands)
    return jnp.transpose(products, (1, 0, 2, 3))


def solution(mesh):
    placed = (P("ka", None, "pw", None), P("ka"), P())
    return jax.shard_map(
        on_device, mesh=mesh, in_specs=placed, out_specs=P("pw", "ka", None, None), check_vma=False
    )
```
